32 devices in a mesh: group: 2 (over y), dp: 8 (over z, x), tensor: 2 (over core).
Axes of the slice: x: 2, y: 2, z: 4, core: 2. Of those that a mesh axis runs over, the one named last changes fastest.
Arguments:
- inputs: bfloat16 [12288, 1536], P(('group', 'dp')), may hold values from -6 to 6
- cotangent: bfloat16 [12288, 1536], P(('group', 'dp')), may hold values from -6 to 6
- lengths: int32 [16, 3], P(('group', 'dp')), may hold values from 1 to 576, 768 in all within a row
- attn_gain: bfloat16 [1536], P('dp'), may hold values from 0.25 to 1.75
- w_query: bfloat16 [1536, 1536], P('dp', 'tensor'), may hold values from -0.15625 to 0.15625
- b_query: bfloat16 [1536], P('tensor'), may hold values from -3 to 3
- w_key: bfloat16 [1536, 256], P('dp', 'tensor'), may hold values from -0.15625 to 0.15625
- b_key: bfloat16 [256], P('tensor'), may hold values from -3 to 3
- w_value: bfloat16 [1536, 256], P('dp', 'tensor'), may hold values from -0.15625 to 0.15625
- b_value: bfloat16 [256], P('tensor'), may hold values from -3 to 3
- w_out: bfloat16 [1536, 1536], P('dp', 'tensor'), may hold values from -1.25 to 1.25
- ffn_gain: bfloat16 [1536], P('dp'), may hold values from 0.25 to 1.75
- w_gate: bfloat16 [1536, 8960], P('dp', 'tensor'), may hold values from -0.15625 to 0.15625
- w_up: bfloat16 [1536, 8960], P('dp', 'tensor'), may hold values from -0.15625 to 0.15625
- w_down: bfloat16 [1536, 8960], P('dp', 'tensor'), may hold values from -0.0625 to 0.0625
Outputs:
- layer_out: bfloat16 [12288, 1536], P(('group', 'dp'))
- input_grad: bfloat16 [12288, 1536], P(('group', 'dp'))
- attn_gain_grad: float32 [1536], P('dp')
- w_query_grad: float32 [1536, 1536], P('dp', 'tensor')
- b_query_grad: float32 [1536], P('tensor')
- w_key_grad: float32 [1536, 256], P('dp', 'tensor')
- b_key_grad: float32 [256], P('tensor')
- w_value_grad: float32 [1536, 256], P('dp', 'tensor')
- b_value_grad: float32 [256], P('tensor')
- w_out_grad: float32 [1536, 1536], P('dp', 'tensor')
- ffn_gain_grad: float32 [1536], P('dp')
- w_gate_grad: float32 [1536, 8960], P('dp', 'tensor')
- w_up_grad: float32 [1536, 8960], P('dp', 'tensor')
- w_down_grad: float32 [1536, 8960], P('dp', 'tensor')
The draws below stay inside these ranges and needn't reach their ends.
Inputs may be any that keep to these rules, and one draw needn't show every extreme that they name: In every stream the 3 lengths sum to 768, and the longest is exactly 576.
All inputs are finite; a program needn't handle non-finite values.
Results may differ from the reference program's by a relative error of at most 0.017.
Values may be sent and summed in bfloat16 or wider, within the bound.
No kernel may reach another device: no remote copies, remote signals or barrier semaphores. Data moves between devices by JAX's collectives and lax.ppermute only.
A program may use at most 384 MiB of HBM per device.

```python
import math
import jax
import jax.numpy as jnp
import numpy as np
from jax import lax

D = 1536
HQ = 12
KV = 2
HD = 128
FF = 8960
SEQ = 768
NSEG = 3
STREAMS = 16
TOKENS = 12288


def steps_of(key, shape, cuts, low, top_value):
    gain = 1.0
    for dim, shards_of in cuts:
        heights = jax.random.uniform(jax.random.fold_in(jax.random.fold_in(key, 6), dim), (shards_of,), jnp.float32, low / len(cuts), top_value / len(cuts))
        gain = gain * jnp.repeat(jnp.exp(heights), shape[dim] // shards_of).reshape((-1,) + (1,) * (len(shape) - 1 - dim))
    return gain


def length_profile(number_of, total, bound, slope):
    portions = [(1 << 20) // math.isqrt(rank ** slope) + 1 for rank in range(2, number_of + 1)]
    rest, counts = total - bound - (number_of - 1), [1] * (number_of - 1)
    while rest > 0:
        movable = [i for i in range(number_of - 1) if counts[i] < bound]
        pool, left = sum([portions[i] for i in movable]), rest
        for i in movable:
            extra = min(bound - counts[i], max(1, left * portions[i] // pool), rest)
            counts[i] = counts[i] + extra
            rest = rest - extra
    return np.array([bound] + counts)


def ragged(key, number_of, total, bound, skew):
    if number_of == 2:
        one = jax.random.randint(key, (), max(1, total - bound), min(bound, total - 1) + 1)
        return jnp.stack([one, total - one])
    sizes = jnp.asarray(length_profile(number_of, total, bound, skew), jnp.int32)
    couples = (number_of - 1) // 2
    source_of, taker = sizes[1:1 + 2 * couples:2], sizes[2:2 + 2 * couples:2]
    slack = jnp.minimum(source_of - 1, bound - taker)
    shifted = jax.random.randint(jax.random.fold_in(key, 1), (couples,), 0, 1 << 20) % (slack + 1)
    sizes = sizes.at[1:1 + 2 * couples:2].set(source_of - shifted).at[2:2 + 2 * couples:2].set(taker + shifted)
    return sizes[jax.random.permutation(jax.random.fold_in(key, 2), number_of)]


def bell_draw(key, shape, spread, limit, shards=(), kind=jnp.bfloat16):
    factor_of = steps_of(key, shape, shards, -0.22, 0.18) if shards else 1.0
    drawn = jax.random.normal(key, shape, jnp.float32) * spread * factor_of
    return jnp.minimum(jnp.maximum(drawn, -limit), limit).astype(kind)


def setup_inputs(seed: int = 0) -> dict:
    key_list = jax.random.split(jax.random.key(seed), 16)
    return {
        "inputs": bell_draw(key_list[0], (TOKENS, D), 1.0, 6.0, ((0, 16),)),
        "cotangent": bell_draw(key_list[1], (TOKENS, D), 1.0, 6.0, ((0, 16),)),
        "lengths": jax.vmap(lambda own: ragged(own, NSEG, SEQ, SEQ * 3 // 4, 2))(jax.random.split(key_list[2], STREAMS)).reshape((STREAMS, NSEG)).astype(jnp.int32),
        "attn_gain": jnp.clip(1.0 + 0.15 * jax.random.normal(key_list[3], (D,), jnp.float32), 0.25, 1.75).astype(jnp.bfloat16),
        "w_query": bell_draw(key_list[4], (D, HQ * HD), D ** -0.5, 0.15625, ((0, 8), (1, 2))),
        "b_query": bell_draw(key_list[5], (HQ * HD,), 0.5, 3.0, ((0, 2),)),
        "w_key": bell_draw(key_list[6], (D, KV * HD), D ** -0.5, 0.15625, ((0, 8), (1, 2))),
        "b_key": bell_draw(key_list[7], (KV * HD,), 0.5, 3.0, ((0, 2),)),
        "w_value": bell_draw(key_list[8], (D, KV * HD), D ** -0.5, 0.15625, ((0, 8), (1, 2))),
        "b_value": bell_draw(key_list[9], (KV * HD,), 0.5, 3.0, ((0, 2),)),
        "w_out": bell_draw(key_list[10], (D, HQ * HD), (HQ * HD // 64) ** -0.5, 1.25, ((0, 8), (1, 2))),
        "ffn_gain": jnp.clip(1.0 + 0.15 * jax.random.normal(key_list[11], (D,), jnp.float32), 0.25, 1.75).astype(jnp.bfloat16),
        "w_gate": bell_draw(key_list[12], (D, FF), D ** -0.5, 0.15625, ((0, 8), (1, 2))),
        "w_up": bell_draw(key_list[13], (D, FF), D ** -0.5, 0.15625, ((0, 8), (1, 2))),
        "w_down": bell_draw(key_list[14], (D, FF), FF ** -0.5, 0.0625, ((0, 8), (1, 2))),
    }


EPSILON = 1e-06
THETA = 10000.0
MASKED_SCORE = -1e+30

@jax.custom_vjp
def low(v):
    return lax.optimization_barrier(v.astype(jnp.bfloat16)).astype(jnp.float32)

@jax.custom_vjp
def low_back(v):
    return v

def low_keep(v):
    return (low(v), None)

def low_pass(kept, grad):
    return (grad,)

def back_keep(v):
    return (v, None)

def back_low(kept, grad):
    return (low(grad),)
low.defvjp(low_keep, low_pass)
low_back.defvjp(back_keep, back_low)

def normalize(values):
    return values * lax.rsqrt(lax.optimization_barrier(jnp.mean(values * values, axis=-1, keepdims=True)) + EPSILON)

def rotate(values, cosine, sine_table):
    half_width = values.shape[-1] // 2
    turned = jnp.concatenate([-values[..., half_width:], values[..., :half_width]], axis=-1)
    return values * cosine + turned * sine_table

def layout(lengths):
    segment_ends = jnp.cumsum(lengths, axis=-1).astype(jnp.int32)
    segment_starts = segment_ends - lengths
    places = jnp.arange(SEQ, dtype=jnp.int32)
    segment = lax.optimization_barrier(jnp.sum((places[:, None] >= segment_ends[..., None, :]).astype(jnp.int32), axis=-1))
    choose = segment[..., None] == jnp.arange(NSEG, dtype=jnp.int32)
    picked = lax.optimization_barrier(jnp.sum(jnp.where(choose, segment_starts[..., None, :], 0), axis=-1))
    return (segment, places - picked)

def angles(position):
    frequency = jnp.exp(-(math.log(THETA) * 2.0 / HD) * jnp.arange(HD // 2, dtype=jnp.float32))
    phase_angle = position.astype(jnp.float32)[..., None] * frequency
    phase_angle = jnp.concatenate([phase_angle, phase_angle], axis=-1)
    return (jnp.cos(phase_angle), jnp.sin(phase_angle))

def full_dot(left_side, right_side):
    return jnp.dot(left_side, right_side, precision=lax.Precision.HIGHEST, preferred_element_type=jnp.float32)

def trans_dot(left_side, right_side):
    return lax.dot_general(left_side, right_side, (((1,), (1,)), ((), ())), precision=lax.Precision.HIGHEST, preferred_element_type=jnp.float32)

def attend(packed):
    queries, keys_rot, values_low, segment = packed
    raw_scores = jnp.einsum('qkgd,skd->kgqs', queries, keys_rot, precision=lax.Precision.HIGHEST)
    scores = low_back(raw_scores * HD ** (-0.5))
    places = jnp.arange(SEQ, dtype=jnp.int32)
    allowed = (segment[:, None] == segment[None, :]) & (places[None, :] <= places[:, None])
    masked = jnp.where(allowed, scores, MASKED_SCORE)
    row_max = lax.optimization_barrier(jnp.max(masked, axis=-1, keepdims=True))
    exp_terms = jnp.exp(masked - row_max)
    probabilities = low(exp_terms / lax.optimization_barrier(jnp.sum(exp_terms, axis=-1, keepdims=True)))
    result = jnp.einsum('kgqs,skd->qkgd', probabilities, values_low, precision=lax.Precision.HIGHEST)
    return result.reshape(SEQ, HQ * HD)

def reference(inputs, cotangent, lengths, attn_gain, w_query, b_query, w_key, b_key, w_value, b_value, w_out, ffn_gain, w_gate, w_up, w_down):
    segment, position = layout(lengths)
    cosine, sine_table = angles(position.reshape(TOKENS))
    cosine = cosine[:, None, :]
    sine_table = sine_table[:, None, :]
    group_size = HQ // KV

    def forward(stream, gain_one, query_w, query_b, key_w, key_b, value_w, value_b, out_w, gain_two, gate_w, up_w, down_w):
        h_one = low(normalize(stream) * gain_one)
        query_pre = low_back(full_dot(h_one, query_w) + query_b).reshape(TOKENS, HQ, HD)
        key_pre = low_back(full_dot(h_one, key_w) + key_b).reshape(TOKENS, KV, HD)
        values_low = low(low_back(full_dot(h_one, value_w) + value_b)).reshape(STREAMS, SEQ, KV, HD)
        queries = low(rotate(query_pre, cosine, sine_table)).reshape(STREAMS, SEQ, KV, group_size, HD)
        keys_rot = low(rotate(key_pre, cosine, sine_table)).reshape(STREAMS, SEQ, KV, HD)
        attended = lax.map(jax.checkpoint(attend), (queries, keys_rot, values_low, segment))
        attended = low(low_back(attended.reshape(TOKENS, HQ * HD)))
        branch = low_back(trans_dot(attended, out_w))
        residual = stream + branch
        h_two = low(normalize(residual) * gain_two)
        gate_pre = low_back(full_dot(h_two, gate_w))
        up_pre = low_back(full_dot(h_two, up_w))
        hidden = low(jax.nn.silu(gate_pre) * up_pre)
        return residual + low_back(trans_dot(hidden, down_w))
    params = [inputs, attn_gain, w_query, b_query, w_key, b_key, w_value, b_value, w_out, ffn_gain, w_gate, w_up, w_down]
    params = [item.astype(jnp.float32) for item in params]
    result, pullback = jax.vjp(forward, *params)
    grads = pullback(cotangent.astype(jnp.float32))
    return (result.astype(jnp.bfloat16), grads[0].astype(jnp.bfloat16), grads[1], grads[2], grads[3], grads[4], grads[5], grads[6], grads[7], grads[8], grads[9], grads[10], grads[11], grads[12])
```

```python
import math

import jax
import jax.numpy as jnp
from jax import lax
from jax.sharding import PartitionSpec as P

HD = 128
SEQ = 768
NSEG = 3


EPSILON = 1e-06
THETA = 10000.0
MASKED_SCORE = -1e30


def normalize(values):
    return values * lax.rsqrt(jnp.mean(values * values, axis=-1, keepdims=True) + EPSILON)


def scaled_norm(values, gain_vec):
    return normalize(values) * gain_vec


def rotate(values, cosine, sine_table):
    half_width = values.shape[-1] // 2
    turned = jnp.concatenate([-values[..., half_width:], values[..., :half_width]], axis=-1)
    return values * cosine + turned * sine_table


def unrotate(values, cosine, sine_table):
    half_width = values.shape[-1] // 2
    sined = values * sine_table
    turned = jnp.concatenate([sined[..., half_width:], -sined[..., :half_width]], axis=-1)
    return values * cosine + turned


def layout(lengths):
    segment_ends = jnp.cumsum(lengths, axis=-1)
    segment_starts = segment_ends - lengths
    places = jnp.arange(SEQ, dtype=jnp.int32)
    segment = jnp.sum((places[:, None] >= segment_ends[..., None, :]).astype(jnp.int32), axis=-1)
    choose = segment[..., None] == jnp.arange(NSEG, dtype=jnp.int32)
    picked = jnp.sum(jnp.where(choose, segment_starts[..., None, :], 0), axis=-1)
    return (segment, places - picked)


def angles(position):
    frequency = jnp.exp(-(math.log(THETA) * 2.0 / HD) * jnp.arange(HD // 2, dtype=jnp.float32))
    phase_angle = position.astype(jnp.float32)[..., None] * frequency
    phase_angle = jnp.concatenate([phase_angle, phase_angle], axis=-1)
    return (jnp.cos(phase_angle), jnp.sin(phase_angle))


def plain_dot(left_side, right_side):
    return jnp.dot(left_side, right_side, preferred_element_type=jnp.float32)


def trans_dot(left_side, right_side):
    return lax.dot_general(
        left_side, right_side, (((1,), (1,)), ((), ())), preferred_element_type=jnp.float32
    )


def outer_dot(left_side, right_side):
    return lax.dot_general(
        left_side, right_side, (((0,), (0,)), ((), ())), preferred_element_type=jnp.float32
    )


def masked_scores(queries, keys_rot, allowed):
    raw_scores = jnp.einsum("qkgd,skd->kgqs", queries, keys_rot, preferred_element_type=jnp.float32)
    return jnp.where(allowed, raw_scores * HD ** (-0.5), MASKED_SCORE)


AXES = ("group", "dp", "tensor")


def routes(dp_count):
    def table(move):
        flat = lambda g, d, t: (g * dp_count + d) * 2 + t
        return [
            (flat(g, d, t), flat(*move(g, d, t)))
            for g in range(2)
            for d in range(dp_count)
            for t in range(2)
        ]

    return {
        "x": table(lambda g, d, t: (g, d ^ 1, t)),
        "y": table(lambda g, d, t: (g ^ 1, d, t)),
        "t": table(lambda g, d, t: (g, d, t ^ 1)),
        "first": table(lambda g, d, t: (g, d ^ 1, t) if t == 0 else (g ^ 1, d, t)),
        "second": table(lambda g, d, t: (g ^ 1, d, t) if t == 0 else (g, d ^ 1, t)),
    }


def local(
    inputs,
    cotangent,
    lengths,
    attn_gain,
    w_query,
    b_query,
    w_key,
    b_key,
    w_value,
    b_value,
    w_out,
    ffn_gain,
    w_gate,
    w_up,
    w_down,
):
    bf16 = jnp.bfloat16
    f32 = jnp.float32
    dp_count = lax.axis_size("dp")
    line = dp_count // 2
    dp_index = lax.axis_index("dp")
    x_index = dp_index % 2
    y_index = lax.axis_index("group")
    core = lax.axis_index("tensor")
    table = routes(dp_count)
    line_groups = [[2 * z + x for z in range(line)] for x in range(2)]
    tokens, d_model = inputs.shape
    half = tokens // 2
    rows = w_query.shape[0]
    head_count = w_query.shape[1] // HD
    kv_count = w_key.shape[1] // HD
    group_size = head_count // kv_count
    ffn_cols = w_gate.shape[1]
    quarter = -(-ffn_cols // 512) * 128
    score_scale = HD ** (-0.5)

    def send(value, route):
        return lax.ppermute(value, AXES, table[route])

    def pick(value, index):
        return lax.dynamic_index_in_dim(value, index, 0, keepdims=False)

    def in_order(index, mine, other):
        first = index == 0
        return jnp.where(first, mine, other), jnp.where(first, other, mine)

    def my_half(value):
        return pick(value.reshape(2, half, value.shape[-1]), core)

    def other_half(value):
        return pick(value.reshape(2, half, value.shape[-1]), 1 - core)

    def both_halves(mine):
        return jnp.concatenate(in_order(core, mine, send(mine, "t")), axis=0)

    def square_gather(mine):
        near = send(mine, "first")
        mine_sib = send(mine, "t")
        far = send(jnp.stack([mine, near]), "second")
        near_sib = send(near, "t")
        far_sib = send(far, "t")
        return jnp.concatenate(
            [mine, near, far[0], far[1], mine_sib, near_sib, far_sib[0], far_sib[1]], axis=0
        )

    def square_scatter(mine, theirs):
        came = send(theirs.astype(bf16), "t")
        total = (mine.astype(f32) + came.astype(f32)).reshape(4, half, d_model)
        came = send(total[2:].astype(bf16), "second")
        total = total[:2] + came.astype(f32)
        came = send(total[1].astype(bf16), "first")
        return total[0] + came.astype(f32)

    def ffn_gather(weight):
        padded = jnp.pad(weight, ((0, 0), (0, 4 * quarter - ffn_cols)))
        parts = padded.reshape(rows, 4, quarter).transpose(1, 0, 2)
        mine = pick(parts, x_index * 2 + y_index)
        came = send(pick(parts, (1 - x_index) * 2 + y_index), "x")
        pair = jnp.stack(in_order(x_index, mine, came))
        full = lax.all_gather(pair, "dp", axis=0, axis_index_groups=line_groups)
        return full.reshape(d_model, quarter)

    def ffn_scatter(grad):
        parts = grad.astype(bf16).reshape(line, 2 * rows, quarter)
        summed = lax.psum_scatter(
            parts, "dp", scatter_dimension=0, axis_index_groups=line_groups
        ).reshape(2, rows, quarter)
        came = send(pick(summed, 1 - x_index), "x")
        pair = jnp.stack(in_order(x_index, pick(summed, x_index), came))
        low, high = in_order(y_index, pair, send(pair, "y"))
        whole = jnp.concatenate([low[0], high[0], low[1], high[1]], axis=1)
        return whole[:, :ffn_cols].astype(f32)

    def attn_scatter(grad):
        summed = lax.psum_scatter(
            grad.astype(bf16), "dp", scatter_dimension=0, tiled=True
        )
        return summed.astype(f32) + send(summed, "y").astype(f32)

    stream = inputs.astype(f32)
    segment, position = layout(lengths[0])
    cosine, sine_table = angles(position)
    cosine = cosine[:, None, :]
    sine_table = sine_table[:, None, :]
    places = jnp.arange(SEQ, dtype=jnp.int32)
    allowed = (segment[:, None] == segment[None, :]) & (places[None, :] <= places[:, None])

    gains = jnp.pad(
        jnp.stack([attn_gain, ffn_gain], axis=1), ((0, 0), (0, 126))
    )
    query_cols = head_count * HD
    key_cols = kv_count * HD
    qkv_cols = query_cols + 2 * key_cols
    qkv_full = lax.all_gather(
        jnp.concatenate([w_query, w_key, w_value, gains], axis=1), "dp", axis=0, tiled=True
    )
    out_full = lax.all_gather(w_out, "dp", axis=0, tiled=True)
    gate_full = ffn_gather(w_gate)
    up_full = ffn_gather(w_up)
    down_full = ffn_gather(w_down)
    cot_half = my_half(cotangent)
    cot_all = square_gather(cot_half)

    gain_one = qkv_full[:, qkv_cols].astype(f32)
    gain_two = qkv_full[:, qkv_cols + 1].astype(f32)
    qkv_full = qkv_full[:, :qkv_cols]

    inv_one = lax.rsqrt(jnp.mean(stream * stream, axis=-1, keepdims=True) + EPSILON)
    h_one = (stream * inv_one * gain_one).astype(bf16)
    qkv_bias = jnp.concatenate([b_query, b_key, b_value]).astype(f32)
    qkv_pre = plain_dot(h_one, qkv_full) + qkv_bias
    query_pre = qkv_pre[:, :query_cols]
    key_pre = qkv_pre[:, query_cols : query_cols + key_cols]
    value_pre = qkv_pre[:, query_cols + key_cols :]
    queries = rotate(query_pre.reshape(SEQ, head_count, HD), cosine, sine_table).astype(bf16)
    queries = queries.reshape(SEQ, kv_count, group_size, HD)
    keys_rot = rotate(key_pre.reshape(SEQ, kv_count, HD), cosine, sine_table).astype(bf16)
    values_low = value_pre.astype(bf16).reshape(SEQ, kv_count, HD)
    scores = masked_scores(queries, keys_rot, allowed)
    row_max = jnp.max(scores, axis=-1, keepdims=True)
    exp_terms = jnp.exp(scores - row_max)
    row_total = jnp.sum(exp_terms, axis=-1, keepdims=True)
    log_total = row_max + jnp.log(row_total)
    probs_low = (exp_terms / row_total).astype(bf16)
    attended = jnp.einsum("kgqs,skd->qkgd", probs_low, values_low, preferred_element_type=f32)
    attended = attended.reshape(SEQ, head_count * HD).astype(bf16)
    branch = trans_dot(attended, out_full)
    resid = (
        my_half(stream)
        + my_half(branch)
        + send(other_half(branch).astype(bf16), "t").astype(f32)
    )
    inv_two = lax.rsqrt(jnp.mean(resid * resid, axis=-1, keepdims=True) + EPSILON)
    norm_two = resid * inv_two
    h_two = square_gather((norm_two * gain_two).astype(bf16))

    gate_pre = plain_dot(h_two, gate_full)
    up_pre = plain_dot(h_two, up_full)
    sigmoid_gate = jax.nn.sigmoid(gate_pre)
    swish_gate = gate_pre * sigmoid_gate
    hidden = (swish_gate * up_pre).astype(bf16)
    down_grad = ffn_scatter(outer_dot(cot_all, hidden))
    d_hidden = plain_dot(cot_all, down_full)
    d_gate = (d_hidden * up_pre * sigmoid_gate * (1.0 + gate_pre * (1.0 - sigmoid_gate))).astype(
        bf16
    )
    d_up = (d_hidden * swish_gate).astype(bf16)
    mid = 4 * half

    def entry(part):
        return trans_dot(d_gate[part], gate_full) + trans_dot(d_up[part], up_full)

    d_h_two = square_scatter(entry(slice(0, mid)), entry(slice(mid, None)))
    gate_grad = ffn_scatter(outer_dot(h_two, d_gate))
    up_grad = ffn_scatter(outer_dot(h_two, d_up))
    ffn_total = square_scatter(
        trans_dot(hidden[:mid], down_full), trans_dot(hidden[mid:], down_full)
    )
    layer_out = both_halves((resid + ffn_total).astype(bf16))

    scaled = d_h_two * gain_two
    d_resid = cot_half.astype(f32) + inv_two * (
        scaled - norm_two * jnp.mean(norm_two * scaled, axis=-1, keepdims=True)
    )
    gain_two_part = jnp.sum(d_h_two * norm_two, axis=0)
    d_out_low = both_halves(d_resid.astype(bf16))
    out_grad = attn_scatter(outer_dot(d_out_low, attended))
    d_attended = (
        plain_dot(d_out_low, out_full).astype(bf16).reshape(SEQ, kv_count, group_size, HD)
    )
    scores = masked_scores(queries, keys_rot, allowed)
    probabilities = jnp.exp(scores - log_total)
    d_probs = jnp.einsum("qkgd,skd->kgqs", d_attended, values_low, preferred_element_type=f32)
    d_value = jnp.einsum(
        "kgqs,qkgd->skd", probabilities.astype(bf16), d_attended, preferred_element_type=f32
    )
    d_value = d_value.reshape(SEQ, kv_count * HD).astype(bf16)
    d_scores = probabilities * (d_probs - jnp.sum(probabilities * d_probs, axis=-1, keepdims=True))
    d_scores = d_scores.astype(bf16)
    d_query_rot = (
        jnp.einsum("kgqs,skd->qkgd", d_scores, keys_rot, preferred_element_type=f32) * score_scale
    )
    d_key_rot = (
        jnp.einsum("kgqs,qkgd->skd", d_scores, queries, preferred_element_type=f32) * score_scale
    )
    d_query = (
        unrotate(d_query_rot.reshape(SEQ, head_count, HD), cosine, sine_table)
        .astype(bf16)
        .reshape(SEQ, head_count * HD)
    )
    d_key = unrotate(d_key_rot, cosine, sine_table).astype(bf16).reshape(SEQ, kv_count * HD)
    d_qkv = jnp.concatenate([d_query, d_key, d_value], axis=1)
    qkv_grad = attn_scatter(outer_dot(h_one, d_qkv))
    entry_one = trans_dot(d_qkv, qkv_full)
    d_h_one = my_half(entry_one) + send(other_half(entry_one).astype(bf16), "t").astype(f32)
    half_inv = my_half(inv_one)
    norm_one = my_half(stream) * half_inv
    scaled = d_h_one * gain_one
    input_grad = both_halves(
        (
            d_resid
            + half_inv * (scaled - norm_one * jnp.mean(norm_one * scaled, axis=-1, keepdims=True))
        ).astype(bf16)
    )
    gain_one_part = jnp.sum(d_h_one * norm_one, axis=0)

    bias_part = jnp.sum(d_qkv.astype(f32), axis=0)
    small = jnp.concatenate([gain_one_part, gain_two_part, bias_part]).reshape(-1, 128)
    small = small + send(small, "y")
    step = 1
    while step < dp_count:
        small = small + lax.ppermute(small, "dp", [(i, i ^ step) for i in range(dp_count)])
        step *= 2
    small = small.reshape(-1)
    gain_sums = small[: 2 * d_model].reshape(2, dp_count, rows)
    mine = lax.dynamic_index_in_dim(gain_sums, dp_index, 1, keepdims=False)
    mine = mine + send(mine, "t")
    bias_sum = small[2 * d_model :]
    return (
        layer_out,
        input_grad,
        mine[0],
        qkv_grad[:, :query_cols],
        bias_sum[:query_cols],
        qkv_grad[:, query_cols : query_cols + key_cols],
        bias_sum[query_cols : query_cols + key_cols],
        qkv_grad[:, query_cols + key_cols :],
        bias_sum[query_cols + key_cols :],
        out_grad,
        mine[1],
        gate_grad,
        up_grad,
        down_grad,
    )


def solution(mesh):
    in_specs = (
        P(("group", "dp"), None),
        P(("group", "dp"), None),
        P(("group", "dp"), None),
        P("dp"),
        P("dp", "tensor"),
        P("tensor"),
        P("dp", "tensor"),
        P("tensor"),
        P("dp", "tensor"),
        P("tensor"),
        P("dp", "tensor"),
        P("dp"),
        P("dp", "tensor"),
        P("dp", "tensor"),
        P("dp", "tensor"),
    )
    out_specs = (
        P(("group", "dp"), None),
        P(("group", "dp"), None),
        P("dp"),
        P("dp", "tensor"),
        P("tensor"),
        P("dp", "tensor"),
        P("tensor"),
        P("dp", "tensor"),
        P("tensor"),
        P("dp", "tensor"),
        P("dp"),
        P("dp", "tensor"),
        P("dp", "tensor"),
        P("dp", "tensor"),
    )
    return jax.shard_map(local, mesh=mesh, in_specs=in_specs, out_specs=out_specs, check_vma=False)
```

```python
import math

import jax
import jax.numpy as jnp
from jax import lax
from jax.sharding import PartitionSpec as P

HD = 128
SEQ = 768
NSEG = 3


EPSILON = 1e-06
THETA = 10000.0
MASKED_SCORE = -1e30


def normalize(values):
    return values * lax.rsqrt(jnp.mean(values * values, axis=-1, keepdims=True) + EPSILON)


def scaled_norm(values, gain_vec):
    return normalize(values) * gain_vec


def rotate(values, cosine, sine_table):
    half_width = values.shape[-1] // 2
    turned = jnp.concatenate([-values[..., half_width:], values[..., :half_width]], axis=-1)
    return values * cosine + turned * sine_table


def unrotate(values, cosine, sine_table):
    half_width = values.shape[-1] // 2
    sined = values * sine_table
    turned = jnp.concatenate([sined[..., half_width:], -sined[..., :half_width]], axis=-1)
    return values * cosine + turned


def layout(lengths):
    segment_ends = jnp.cumsum(lengths, axis=-1)
    segment_starts = segment_ends - lengths
    places = jnp.arange(SEQ, dtype=jnp.int32)
    segment = jnp.sum((places[:, None] >= segment_ends[..., None, :]).astype(jnp.int32), axis=-1)
    choose = segment[..., None] == jnp.arange(NSEG, dtype=jnp.int32)
    picked = jnp.sum(jnp.where(choose, segment_starts[..., None, :], 0), axis=-1)
    return (segment, places - picked)


def angles(position):
    frequency = jnp.exp(-(math.log(THETA) * 2.0 / HD) * jnp.arange(HD // 2, dtype=jnp.float32))
    phase_angle = position.astype(jnp.float32)[..., None] * frequency
    phase_angle = jnp.concatenate([phase_angle, phase_angle], axis=-1)
    return (jnp.cos(phase_angle), jnp.sin(phase_angle))


def plain_dot(left_side, right_side):
    return jnp.dot(left_side, right_side, preferred_element_type=jnp.float32)


def trans_dot(left_side, right_side):
    return lax.dot_general(
        left_side, right_side, (((1,), (1,)), ((), ())), preferred_element_type=jnp.float32
    )


def outer_dot(left_side, right_side):
    return lax.dot_general(
        left_side, right_side, (((0,), (0,)), ((), ())), preferred_element_type=jnp.float32
    )


def masked_scores(queries, keys_rot, allowed):
    raw_scores = jnp.einsum("qkgd,skd->kgqs", queries, keys_rot, preferred_element_type=jnp.float32)
    return jnp.where(allowed, raw_scores * HD ** (-0.5), MASKED_SCORE)


AXES = ("group", "dp", "tensor")


def routes(dp_count):
    def table(move):
        flat = lambda g, d, t: (g * dp_count + d) * 2 + t
        return [
            (flat(g, d, t), flat(*move(g, d, t)))
            for g in range(2)
            for d in range(dp_count)
            for t in range(2)
        ]

    shifts = {
        step: table(lambda g, d, t: (g, (d + 2 * step) % dp_count, t))
        for step in range(1, dp_count // 2)
    }
    return shifts | {
        "x": table(lambda g, d, t: (g, d ^ 1, t)),
        "y": table(lambda g, d, t: (g ^ 1, d, t)),
        "t": table(lambda g, d, t: (g, d, t ^ 1)),
        "first": table(lambda g, d, t: (g, d ^ 1, t) if t == 0 else (g ^ 1, d, t)),
        "second": table(lambda g, d, t: (g ^ 1, d, t) if t == 0 else (g, d ^ 1, t)),
    }


def local(
    inputs,
    cotangent,
    lengths,
    attn_gain,
    w_query,
    b_query,
    w_key,
    b_key,
    w_value,
    b_value,
    w_out,
    ffn_gain,
    w_gate,
    w_up,
    w_down,
):
    bf16 = jnp.bfloat16
    f32 = jnp.float32
    dp_count = lax.axis_size("dp")
    line = dp_count // 2
    dp_index = lax.axis_index("dp")
    x_index = dp_index % 2
    z_index = dp_index // 2
    y_index = lax.axis_index("group")
    core = lax.axis_index("tensor")
    table = routes(dp_count)
    line_groups = [[2 * z + x for z in range(line)] for x in range(2)]
    tokens, d_model = inputs.shape
    half = tokens // 2
    rows = w_query.shape[0]
    head_count = w_query.shape[1] // HD
    kv_count = w_key.shape[1] // HD
    group_size = head_count // kv_count
    ffn_cols = w_gate.shape[1]
    quarter = -(-ffn_cols // 512) * 128
    score_scale = HD ** (-0.5)

    def send(value, route):
        return lax.ppermute(value, AXES, table[route])

    def pick(value, index):
        return lax.dynamic_index_in_dim(value, index, 0, keepdims=False)

    def in_order(index, mine, other):
        first = index == 0
        return jnp.where(first, mine, other), jnp.where(first, other, mine)

    def my_half(value):
        return pick(value.reshape(2, half, value.shape[-1]), core)

    def other_half(value):
        return pick(value.reshape(2, half, value.shape[-1]), 1 - core)

    def both_halves(mine):
        return jnp.concatenate(in_order(core, mine, send(mine, "t")), axis=0)

    def square_gather(mine):
        near = send(mine, "first")
        mine_sib = send(mine, "t")
        far = send(jnp.stack([mine, near]), "second")
        near_sib = send(near, "t")
        far_sib = send(far, "t")
        return jnp.concatenate(
            [mine, near, far[0], far[1], mine_sib, near_sib, far_sib[0], far_sib[1]], axis=0
        )

    def square_scatter(mine, theirs):
        came = send(theirs.astype(bf16), "t")
        total = (mine.astype(f32) + came.astype(f32)).reshape(4, half, d_model)
        came = send(total[2:].astype(bf16), "second")
        total = total[:2] + came.astype(f32)
        came = send(total[1].astype(bf16), "first")
        return total[0] + came.astype(f32)

    def after(value, *others):
        return lax.optimization_barrier((value, *others))[0]

    def ffn_parts(weight):
        padded = jnp.pad(weight, ((0, 0), (0, 4 * quarter - ffn_cols)))
        return padded.reshape(rows, 4, quarter).transpose(1, 0, 2)

    def ffn_pair(parts):
        mine = jnp.concatenate([pick(p, x_index * 2 + y_index) for p in parts], axis=1)
        other = jnp.concatenate([pick(p, (1 - x_index) * 2 + y_index) for p in parts], axis=1)
        return jnp.stack(in_order(x_index, mine, send(other, "x")))

    def ffn_gather(pair):
        full = lax.all_gather(pair, "dp", axis=0, axis_index_groups=line_groups)
        return full.reshape(d_model, pair.shape[-1])

    def put(whole, piece, index):
        return lax.dynamic_update_slice(whole, piece.reshape((1,) + piece.shape), index)

    part_rows = rows // 2

    def attn_line(weight):
        mine = lax.dynamic_slice_in_dim(weight, y_index * part_rows, part_rows, 0)
        whole = jnp.zeros((line,) + mine.shape, bf16)
        came = [mine] + [send(mine, step) for step in range(1, line)]
        for step, piece in enumerate(came):
            whole = put(whole, piece, ((z_index - step) % line, 0, 0))
        return whole

    def attn_square(blocks):
        cols = blocks.shape[-1]
        whole = jnp.zeros((line, 2, 2, part_rows, cols), bf16)
        cut = line // 2
        low, high = blocks[:cut], blocks[cut:]
        low_near = send(low, "x")
        high_near = send(high, "y")
        low_far = send(jnp.stack([low, low_near]), "y")
        high_far = send(jnp.stack([high, high_near]), "x")

        def place(whole, piece, z, x, y):
            return lax.dynamic_update_slice(whole, piece[:, None, None], (z, x, y, 0, 0))

        x, y = x_index, y_index
        whole = place(whole, low, 0, x, y)
        whole = place(whole, low_near, 0, 1 - x, y)
        whole = place(whole, low_far[0], 0, x, 1 - y)
        whole = place(whole, low_far[1], 0, 1 - x, 1 - y)
        whole = place(whole, high, cut, x, y)
        whole = place(whole, high_near, cut, x, 1 - y)
        whole = place(whole, high_far[0], cut, 1 - x, y)
        whole = place(whole, high_far[1], cut, 1 - x, 1 - y)
        return whole.reshape(d_model, cols)

    def ffn_scatter(grad):
        parts = grad.astype(bf16).reshape(line, 2 * rows, quarter)
        return lax.psum_scatter(
            parts, "dp", scatter_dimension=0, axis_index_groups=line_groups
        ).reshape(2, rows, quarter)

    def ffn_swap(summed):
        came = send(pick(summed, 1 - x_index), "x")
        pair = jnp.stack(in_order(x_index, pick(summed, x_index), came))
        low, high = in_order(y_index, pair, send(pair, "y"))
        whole = jnp.concatenate([low[0], high[0], low[1], high[1]], axis=1)
        return whole[:, :ffn_cols].astype(f32)

    def attn_scatter(grad):
        cols = grad.shape[-1]
        cut = line // 2
        view = grad.astype(bf16).reshape(line, 2, 2, part_rows, cols)

        def take(value, axis, index):
            return lax.dynamic_index_in_dim(value, index, axis, keepdims=False)

        low, high = view[:cut], view[cut:]
        low = take(low, 1, x_index).astype(f32) + send(take(low, 1, 1 - x_index), "x").astype(f32)
        high = take(high, 2, y_index).astype(f32) + send(take(high, 2, 1 - y_index), "y").astype(f32)
        low, high = low.astype(bf16), high.astype(bf16)
        low = take(low, 1, y_index).astype(f32) + send(take(low, 1, 1 - y_index), "y").astype(f32)
        high = take(high, 1, x_index).astype(f32) + send(take(high, 1, 1 - x_index), "x").astype(f32)
        blocks = jnp.concatenate([low, high]).astype(bf16)
        total = pick(blocks, z_index).astype(f32)
        for step in range(1, line):
            total = total + send(pick(blocks, (z_index + step) % line), step).astype(f32)
        mine = total.astype(bf16)
        return jnp.concatenate(in_order(y_index, mine, send(mine, "y"))).astype(f32)

    stream = inputs.astype(f32)
    segment, position = layout(lengths[0])
    cosine, sine_table = angles(position)
    cosine = cosine[:, None, :]
    sine_table = sine_table[:, None, :]
    places = jnp.arange(SEQ, dtype=jnp.int32)
    allowed = (segment[:, None] == segment[None, :]) & (places[None, :] <= places[:, None])

    gains = jnp.pad(
        jnp.stack([attn_gain, ffn_gain], axis=1), ((0, 0), (0, 126))
    )
    query_cols = head_count * HD
    key_cols = kv_count * HD
    qkv_cols = query_cols + 2 * key_cols
    gate_up_pair = ffn_pair([ffn_parts(w_gate), ffn_parts(w_up)])
    qkv_line = attn_line(jnp.concatenate([w_query, w_key, w_value, gains], axis=1))
    out_line = attn_line(after(w_out, qkv_line))
    qkv_full = attn_square(after(qkv_line, gate_up_pair))
    out_full = attn_square(after(out_line, qkv_full))
    down_pair = ffn_pair([ffn_parts(after(w_down, qkv_full))])
    gate_up_full = ffn_gather(gate_up_pair)
    down_full = ffn_gather(after(down_pair, gate_up_pair))
    gate_full = gate_up_full[:, :quarter]
    up_full = gate_up_full[:, quarter:]
    cot_half = my_half(cotangent)
    cot_all = square_gather(after(cot_half, out_full))

    gain_one = qkv_full[:, qkv_cols].astype(f32)
    gain_two = qkv_full[:, qkv_cols + 1].astype(f32)
    qkv_full = qkv_full[:, :qkv_cols]

    inv_one = lax.rsqrt(jnp.mean(stream * stream, axis=-1, keepdims=True) + EPSILON)
    h_one = (stream * inv_one * gain_one).astype(bf16)
    qkv_bias = jnp.concatenate([b_query, b_key, b_value]).astype(f32)
    qkv_pre = plain_dot(h_one, qkv_full) + qkv_bias
    query_pre = qkv_pre[:, :query_cols]
    key_pre = qkv_pre[:, query_cols : query_cols + key_cols]
    value_pre = qkv_pre[:, query_cols + key_cols :]
    queries = rotate(query_pre.reshape(SEQ, head_count, HD), cosine, sine_table).astype(bf16)
    queries = queries.reshape(SEQ, kv_count, group_size, HD)
    keys_rot = rotate(key_pre.reshape(SEQ, kv_count, HD), cosine, sine_table).astype(bf16)
    values_low = value_pre.astype(bf16).reshape(SEQ, kv_count, HD)
    scores = masked_scores(queries, keys_rot, allowed)
    row_max = jnp.max(scores, axis=-1, keepdims=True)
    exp_terms = jnp.exp(scores - row_max)
    row_total = jnp.sum(exp_terms, axis=-1, keepdims=True)
    log_total = row_max + jnp.log(row_total)
    probs_low = (exp_terms / row_total).astype(bf16)
    attended = jnp.einsum("kgqs,skd->qkgd", probs_low, values_low, preferred_element_type=f32)
    attended = attended.reshape(SEQ, head_count * HD).astype(bf16)
    branch = trans_dot(attended, out_full)
    resid = (
        my_half(stream)
        + my_half(branch)
        + send(other_half(branch).astype(bf16), "t").astype(f32)
    )
    inv_two = lax.rsqrt(jnp.mean(resid * resid, axis=-1, keepdims=True) + EPSILON)
    norm_two = resid * inv_two
    h_two = square_gather((norm_two * gain_two).astype(bf16))

    gate_pre = plain_dot(h_two, gate_full)
    up_pre = plain_dot(h_two, up_full)
    sigmoid_gate = jax.nn.sigmoid(gate_pre)
    swish_gate = gate_pre * sigmoid_gate
    hidden = (swish_gate * up_pre).astype(bf16)
    down_sum = ffn_scatter(outer_dot(cot_all, hidden))
    d_hidden = plain_dot(cot_all, down_full)
    d_gate = (d_hidden * up_pre * sigmoid_gate * (1.0 + gate_pre * (1.0 - sigmoid_gate))).astype(
        bf16
    )
    d_up = (d_hidden * swish_gate).astype(bf16)
    mid = 4 * half

    def entry(part):
        return trans_dot(d_gate[part], gate_full) + trans_dot(d_up[part], up_full)

    d_h_two = square_scatter(entry(slice(0, mid)), entry(slice(mid, None)))
    gate_sum = ffn_scatter(outer_dot(h_two, d_gate))
    up_sum = ffn_scatter(outer_dot(h_two, d_up))
    ffn_total = square_scatter(
        trans_dot(hidden[:mid], down_full), trans_dot(hidden[mid:], down_full)
    )
    layer_out = both_halves((resid + ffn_total).astype(bf16))

    scaled = d_h_two * gain_two
    d_resid = cot_half.astype(f32) + inv_two * (
        scaled - norm_two * jnp.mean(norm_two * scaled, axis=-1, keepdims=True)
    )
    gain_two_part = jnp.sum(d_h_two * norm_two, axis=0)
    d_out_low = both_halves(d_resid.astype(bf16))
    out_grad = attn_scatter(outer_dot(d_out_low, attended))
    d_attended = (
        plain_dot(d_out_low, out_full).astype(bf16).reshape(SEQ, kv_count, group_size, HD)
    )
    scores = masked_scores(queries, keys_rot, allowed)
    probabilities = jnp.exp(scores - log_total)
    d_probs = jnp.einsum("qkgd,skd->kgqs", d_attended, values_low, preferred_element_type=f32)
    d_value = jnp.einsum(
        "kgqs,qkgd->skd", probabilities.astype(bf16), d_attended, preferred_element_type=f32
    )
    d_value = d_value.reshape(SEQ, kv_count * HD).astype(bf16)
    d_scores = probabilities * (d_probs - jnp.sum(probabilities * d_probs, axis=-1, keepdims=True))
    d_scores = d_scores.astype(bf16)
    d_query_rot = (
        jnp.einsum("kgqs,skd->qkgd", d_scores, keys_rot, preferred_element_type=f32) * score_scale
    )
    d_key_rot = (
        jnp.einsum("kgqs,qkgd->skd", d_scores, queries, preferred_element_type=f32) * score_scale
    )
    d_query = (
        unrotate(d_query_rot.reshape(SEQ, head_count, HD), cosine, sine_table)
        .astype(bf16)
        .reshape(SEQ, head_count * HD)
    )
    d_key = unrotate(d_key_rot, cosine, sine_table).astype(bf16).reshape(SEQ, kv_count * HD)
    d_qkv = jnp.concatenate([d_query, d_key, d_value], axis=1)
    qkv_grad = attn_scatter(outer_dot(h_one, d_qkv))
    entry_one = trans_dot(d_qkv, qkv_full)
    down_grad = ffn_swap(after(down_sum, d_out_low))
    gate_grad = ffn_swap(after(gate_sum, entry_one))
    up_grad = ffn_swap(after(up_sum, qkv_grad))
    d_h_one = my_half(entry_one) + send(other_half(entry_one).astype(bf16), "t").astype(f32)
    half_inv = my_half(inv_one)
    norm_one = my_half(stream) * half_inv
    scaled = d_h_one * gain_one
    input_grad = both_halves(
        (
            d_resid
            + half_inv * (scaled - norm_one * jnp.mean(norm_one * scaled, axis=-1, keepdims=True))
        ).astype(bf16)
    )
    gain_one_part = jnp.sum(d_h_one * norm_one, axis=0)

    bias_part = jnp.sum(d_qkv.astype(f32), axis=0)
    small = jnp.concatenate([gain_one_part, gain_two_part, bias_part]).reshape(-1, 128)
    small = small + send(small, "y")
    step = 1
    while step < dp_count:
        small = small + lax.ppermute(small, "dp", [(i, i ^ step) for i in range(dp_count)])
        step *= 2
    small = small.reshape(-1)
    gain_sums = small[: 2 * d_model].reshape(2, dp_count, rows)
    mine = lax.dynamic_index_in_dim(gain_sums, dp_index, 1, keepdims=False)
    mine = mine + send(mine, "t")
    bias_sum = small[2 * d_model :]
    return (
        layer_out,
        input_grad,
        mine[0],
        qkv_grad[:, :query_cols],
        bias_sum[:query_cols],
        qkv_grad[:, query_cols : query_cols + key_cols],
        bias_sum[query_cols : query_cols + key_cols],
        qkv_grad[:, query_cols + key_cols :],
        bias_sum[query_cols + key_cols :],
        out_grad,
        mine[1],
        gate_grad,
        up_grad,
        down_grad,
    )


def solution(mesh):
    in_specs = (
        P(("group", "dp"), None),
        P(("group", "dp"), None),
        P(("group", "dp"), None),
        P("dp"),
        P("dp", "tensor"),
        P("tensor"),
        P("dp", "tensor"),
        P("tensor"),
        P("dp", "tensor"),
        P("tensor"),
        P("dp", "tensor"),
        P("dp"),
        P("dp", "tensor"),
        P("dp", "tensor"),
        P("dp", "tensor"),
    )
    out_specs = (
        P(("group", "dp"), None),
        P(("group", "dp"), None),
        P("dp"),
        P("dp", "tensor"),
        P("tensor"),
        P("dp", "tensor"),
        P("tensor"),
        P("dp", "tensor"),
        P("tensor"),
        P("dp", "tensor"),
        P("dp"),
        P("dp", "tensor"),
        P("dp", "tensor"),
        P("dp", "tensor"),
    )
    return jax.shard_map(local, mesh=mesh, in_specs=in_specs, out_specs=out_specs, check_vma=False)
```

```python
import math

import jax
import jax.numpy as jnp
from jax import lax
from jax.experimental import pallas as pl
from jax.experimental.pallas import tpu as pltpu
from jax.sharding import PartitionSpec as P

HD = 128
SEQ = 768
NSEG = 3


EPSILON = 1e-06
THETA = 10000.0
MASKED_SCORE = -1e30


def layout(lengths):
    segment_ends = jnp.cumsum(lengths, axis=-1)
    segment_starts = segment_ends - lengths
    places = jnp.arange(SEQ, dtype=jnp.int32)
    segment = jnp.sum((places[:, None] >= segment_ends[..., None, :]).astype(jnp.int32), axis=-1)
    choose = segment[..., None] == jnp.arange(NSEG, dtype=jnp.int32)
    picked = jnp.sum(jnp.where(choose, segment_starts[..., None, :], 0), axis=-1)
    return (segment, places - picked)


def angles(position):
    frequency = jnp.exp(-(math.log(THETA) * 2.0 / HD) * jnp.arange(HD // 2, dtype=jnp.float32))
    phase_angle = position.astype(jnp.float32)[..., None] * frequency
    phase_angle = jnp.concatenate([phase_angle, phase_angle], axis=-1)
    return (jnp.cos(phase_angle), jnp.sin(phase_angle))


def plain_dot(left_side, right_side):
    return jnp.dot(left_side, right_side, preferred_element_type=jnp.float32)


def trans_dot(left_side, right_side):
    return lax.dot_general(
        left_side, right_side, (((1,), (1,)), ((), ())), preferred_element_type=jnp.float32
    )


def outer_dot(left_side, right_side):
    return lax.dot_general(
        left_side, right_side, (((0,), (0,)), ((), ())), preferred_element_type=jnp.float32
    )


BLOCK = 256


def rotated(values, cosine, signed_sine):
    return values * cosine + pltpu.roll(values, HD // 2, 1) * signed_sine


def unrotated(values, cosine, signed_sine):
    return values * cosine - pltpu.roll(values, HD // 2, 1) * signed_sine


def allowed_block(start, top, width):
    row = top + lax.broadcasted_iota(jnp.int32, (BLOCK, width), 0)
    col = lax.broadcasted_iota(jnp.int32, (BLOCK, width), 1)
    return (col >= start) & (col <= row)


def attend_body(
    q_pre, k_pre, v_pre, cosine, signed_sine, start, q_out, k_out, v_out, att_out, lse_out
):
    head = pl.program_id(0)

    @pl.when(head == 0)
    def _():
        k_out[...] = rotated(k_pre[...], cosine[...], signed_sine[...]).astype(jnp.bfloat16)
        v_out[...] = v_pre[...].astype(jnp.bfloat16)
        lse_out[...] = jnp.zeros_like(lse_out)

    q_out[...] = rotated(q_pre[...], cosine[...], signed_sine[...]).astype(jnp.bfloat16)
    for top in range(0, SEQ, BLOCK):
        width = top + BLOCK
        rows = pl.ds(top, BLOCK)
        scores = trans_dot(q_out[rows, :], k_out[:width, :]) * HD ** (-0.5)
        scores = jnp.where(allowed_block(start[rows, :], top, width), scores, MASKED_SCORE)
        row_max = jnp.max(scores, axis=1, keepdims=True)
        terms = jnp.exp(scores - row_max)
        total = jnp.sum(terms, axis=1, keepdims=True)
        probs = (terms * (1.0 / total)).astype(jnp.bfloat16)
        att_out[rows, :] = plain_dot(probs, v_out[:width, :]).astype(jnp.bfloat16)
        lane = lax.broadcasted_iota(jnp.int32, (BLOCK, HD), 1)
        lse_out[rows, :] = jnp.where(lane == head, row_max + jnp.log(total), lse_out[rows, :])


def attend_back_body(
    q_rot, k_rot, v_low, d_att, lse, cosine, signed_sine, start, grad_out, dk_sum, dv_sum
):
    head = pl.program_id(0)

    @pl.when(head == 0)
    def _():
        dk_sum[...] = jnp.zeros_like(dk_sum)
        dv_sum[...] = jnp.zeros_like(dv_sum)

    for top in range(0, SEQ, BLOCK):
        width = top + BLOCK
        rows = pl.ds(top, BLOCK)
        query = q_rot[rows, :]
        d_out = d_att[rows, :]
        lane = lax.broadcasted_iota(jnp.int32, (BLOCK, HD), 1)
        row_lse = jnp.sum(jnp.where(lane == head, lse[rows, :], 0.0), axis=1, keepdims=True)
        scores = trans_dot(query, k_rot[:width, :]) * HD ** (-0.5)
        scores = jnp.where(allowed_block(start[rows, :], top, width), scores, MASKED_SCORE)
        probs = jnp.exp(scores - row_lse)
        d_probs = trans_dot(d_out, v_low[:width, :])
        inner = jnp.sum(probs * d_probs, axis=1, keepdims=True)
        d_scores = (probs * (d_probs - inner)).astype(jnp.bfloat16)
        d_query = plain_dot(d_scores, k_rot[:width, :]) * HD ** (-0.5)
        d_query = unrotated(d_query, cosine[rows, :], signed_sine[rows, :])
        cols = pl.ds(pl.multiple_of(head * HD, HD), HD)
        grad_out[rows, cols] = d_query.astype(jnp.bfloat16)
        dk_sum[:width, :] += outer_dot(d_scores, query)
        dv_sum[:width, :] += outer_dot(probs.astype(jnp.bfloat16), d_out)

    @pl.when(head == pl.num_programs(0) - 1)
    def _():
        edge = grad_out.shape[1] - 2 * HD
        d_key = unrotated(dk_sum[...] * HD ** (-0.5), cosine[...], signed_sine[...])
        grad_out[:, edge : edge + HD] = d_key.astype(jnp.bfloat16)
        grad_out[:, edge + HD :] = dv_sum[...].astype(jnp.bfloat16)


def fixed(shape):
    return pl.BlockSpec(shape, lambda head: (0, 0))


def column(index):
    return pl.BlockSpec((SEQ, HD), lambda head: (0, index))


PER_HEAD = pl.BlockSpec((SEQ, HD), lambda head: (0, head))
WHOLE = (SEQ, HD)


def attend(qkv_pre, cosine, signed_sine, start):
    heads = qkv_pre.shape[1] // HD - 2
    shape = lambda cols, kind: jax.ShapeDtypeStruct((SEQ, cols), kind)
    low = jnp.bfloat16
    return pl.pallas_call(
        attend_body,
        grid=(heads,),
        in_specs=[PER_HEAD, column(heads), column(heads + 1)]
        + [fixed(WHOLE), fixed(WHOLE), fixed((SEQ, 1))],
        out_specs=[PER_HEAD, fixed(WHOLE), fixed(WHOLE), PER_HEAD, fixed(WHOLE)],
        out_shape=[
            shape(heads * HD, low),
            shape(HD, low),
            shape(HD, low),
            shape(heads * HD, low),
            shape(HD, jnp.float32),
        ],
    )(qkv_pre, qkv_pre, qkv_pre, cosine, signed_sine, start)


def attend_back(q_rot, k_rot, v_low, d_att, lse, cosine, signed_sine, start):
    heads = q_rot.shape[1] // HD
    cols = (heads + 2) * HD
    return pl.pallas_call(
        attend_back_body,
        grid=(heads,),
        in_specs=[PER_HEAD, fixed(WHOLE), fixed(WHOLE), PER_HEAD, fixed(WHOLE)]
        + [fixed(WHOLE), fixed(WHOLE), fixed((SEQ, 1))],
        out_specs=fixed((SEQ, cols)),
        out_shape=jax.ShapeDtypeStruct((SEQ, cols), jnp.bfloat16),
        scratch_shapes=[pltpu.VMEM(WHOLE, jnp.float32), pltpu.VMEM(WHOLE, jnp.float32)],
    )(q_rot, k_rot, v_low, d_att, lse, cosine, signed_sine, start)


AXES = ("group", "dp", "tensor")


def routes(dp_count):
    def table(move):
        flat = lambda g, d, t: (g * dp_count + d) * 2 + t
        return [
            (flat(g, d, t), flat(*move(g, d, t)))
            for g in range(2)
            for d in range(dp_count)
            for t in range(2)
        ]

    shifts = {
        step: table(lambda g, d, t: (g, (d + 2 * step) % dp_count, t))
        for step in range(1, dp_count // 2)
    }
    return shifts | {
        "x": table(lambda g, d, t: (g, d ^ 1, t)),
        "y": table(lambda g, d, t: (g ^ 1, d, t)),
        "t": table(lambda g, d, t: (g, d, t ^ 1)),
        "first": table(lambda g, d, t: (g, d ^ 1, t) if t == 0 else (g ^ 1, d, t)),
        "second": table(lambda g, d, t: (g ^ 1, d, t) if t == 0 else (g, d ^ 1, t)),
    }


def local(
    inputs,
    cotangent,
    lengths,
    attn_gain,
    w_query,
    b_query,
    w_key,
    b_key,
    w_value,
    b_value,
    w_out,
    ffn_gain,
    w_gate,
    w_up,
    w_down,
):
    bf16 = jnp.bfloat16
    f32 = jnp.float32
    dp_count = lax.axis_size("dp")
    line = dp_count // 2
    dp_index = lax.axis_index("dp")
    x_index = dp_index % 2
    z_index = dp_index // 2
    y_index = lax.axis_index("group")
    core = lax.axis_index("tensor")
    table = routes(dp_count)
    line_groups = [[2 * z + x for z in range(line)] for x in range(2)]
    tokens, d_model = inputs.shape
    half = tokens // 2
    rows = w_query.shape[0]
    head_count = w_query.shape[1] // HD
    kv_count = w_key.shape[1] // HD
    ffn_cols = w_gate.shape[1]
    quarter = -(-ffn_cols // 512) * 128

    def send(value, route):
        return lax.ppermute(value, AXES, table[route])

    def pick(value, index):
        return lax.dynamic_index_in_dim(value, index, 0, keepdims=False)

    def in_order(index, mine, other):
        first = index == 0
        return jnp.where(first, mine, other), jnp.where(first, other, mine)

    def my_half(value):
        return pick(value.reshape(2, half, value.shape[-1]), core)

    def other_half(value):
        return pick(value.reshape(2, half, value.shape[-1]), 1 - core)

    def both_halves(mine):
        return jnp.concatenate(in_order(core, mine, send(mine, "t")), axis=0)

    def after(value, *others):
        return lax.optimization_barrier((value, *others))[0]

    def square_far(mine, near, *others):
        mine_sib = send(mine, "t")
        near_sib = send(near, "t")
        far = send(after(jnp.stack([mine, near]), *others), "second")
        far_sib = send(far, "t")
        whole = jnp.concatenate(
            [mine, near, far[0], far[1], mine_sib, near_sib, far_sib[0], far_sib[1]], axis=0
        )
        return whole, far

    def square_scatter(mine, theirs, *others):
        came = send(theirs, "t")
        total = (mine.astype(f32) + came.astype(f32)).reshape(4, half, d_model)
        came = send(after(total[2:].astype(bf16), *others), "second")
        total = total[:2] + came.astype(f32)
        came = send(total[1].astype(bf16), "first")
        return total[0] + came.astype(f32)

    def ffn_quarter(weight, index):
        parts = [weight[:, i * quarter : (i + 1) * quarter] for i in range(4)]
        parts[3] = jnp.pad(parts[3], ((0, 0), (0, 4 * quarter - ffn_cols)))
        upper = jnp.where(index % 2 == 0, parts[2], parts[3])
        lower = jnp.where(index % 2 == 0, parts[0], parts[1])
        return jnp.where(index < 2, lower, upper)

    def ffn_pair(weights):
        other = [ffn_quarter(w, (1 - x_index) * 2 + y_index) for w in weights]
        came = send(jnp.concatenate(other, axis=1), "x")
        mine = [ffn_quarter(w, x_index * 2 + y_index) for w in weights]
        return jnp.stack(in_order(x_index, jnp.concatenate(mine, axis=1), came))

    def ffn_gather(pair):
        full = lax.all_gather(pair, "dp", axis=0, axis_index_groups=line_groups)
        return full.reshape(d_model, pair.shape[-1])

    def ffn_scatter(grad):
        parts = grad.astype(bf16).reshape(line, 2 * rows, quarter)
        return lax.psum_scatter(
            parts, "dp", scatter_dimension=0, axis_index_groups=line_groups
        ).reshape(2, rows, quarter)

    def ffn_swap(summed):
        came = send(pick(summed, 1 - x_index), "x")
        pair = jnp.stack(in_order(x_index, pick(summed, x_index), came))
        low, high = in_order(y_index, pair, send(pair, "y"))
        whole = jnp.concatenate([low[0], high[0], low[1], high[1]], axis=1)
        return whole[:, :ffn_cols].astype(f32)

    cut = line // 2
    part_rows = rows // 2

    def line_sends(weight):
        mine = lax.dynamic_slice_in_dim(weight, y_index * part_rows, part_rows, 0)
        return [mine] + [send(mine, step) for step in range(1, line)]

    def line_join(pieces):
        whole = jnp.zeros((line,) + pieces[0].shape, bf16)
        for step, piece in enumerate(pieces):
            spot = ((z_index - step) % line, 0, 0)
            whole = lax.dynamic_update_slice(whole, piece[None], spot)
        return whole

    def near_sends(blocks):
        low, high = blocks[:cut], blocks[cut:]
        return low, high, send(low, "x"), send(high, "y")

    def far_join(low, high, low_near, high_near):
        low_far = send(jnp.stack([low, low_near]), "y")
        high_far = send(jnp.stack([high, high_near]), "x")
        cols = low.shape[-1]
        whole = jnp.zeros((line, 2, 2, part_rows, cols), bf16)
        x, y = x_index, y_index
        for piece, z, px, py in (
            (low, 0, x, y),
            (low_near, 0, 1 - x, y),
            (low_far[0], 0, x, 1 - y),
            (low_far[1], 0, 1 - x, 1 - y),
            (high, cut, x, y),
            (high_near, cut, x, 1 - y),
            (high_far[0], cut, 1 - x, y),
            (high_far[1], cut, 1 - x, 1 - y),
        ):
            whole = lax.dynamic_update_slice(whole, piece[:, None, None], (z, px, py, 0, 0))
        return whole.reshape(d_model, cols)

    def take(value, axis, index):
        return lax.dynamic_index_in_dim(value, index, axis, keepdims=False)

    def fold(value, axis, index, route):
        came = send(take(value, axis, 1 - index), route)
        return (take(value, axis, index).astype(f32) + came.astype(f32)).astype(bf16)

    def attn_scatter(grad):
        view = grad.reshape(line, 2, 2, part_rows, grad.shape[-1])
        low = fold(view[:cut], 1, x_index, "x")
        high = fold(view[cut:], 2, y_index, "y")
        low = fold(low, 1, y_index, "y")
        high = fold(high, 1, x_index, "x")
        blocks = jnp.concatenate([low, high])
        total = pick(blocks, z_index).astype(f32)
        for step in range(1, line):
            total = total + send(pick(blocks, (z_index + step) % line), step).astype(f32)
        mine = total.astype(bf16)
        whole = jnp.concatenate(in_order(y_index, mine, send(mine, "y"))).astype(f32)
        return whole, blocks, mine

    query_cols = head_count * HD
    key_cols = kv_count * HD
    qkv_cols = query_cols + 2 * key_cols
    gains = jnp.pad(jnp.stack([attn_gain, ffn_gain], axis=1), ((0, 0), (0, HD - 2)))

    qkv_pieces = line_sends(jnp.concatenate([w_query, w_key, w_value, gains], axis=1))
    gate_up_pair = ffn_pair([w_gate, w_up])
    gate_up_full = ffn_gather(gate_up_pair)
    out_pieces = line_sends(after(w_out, *qkv_pieces))
    qkv_near = near_sends(line_join(qkv_pieces))
    qkv_full = far_join(*qkv_near)
    out_near = near_sends(after(line_join(out_pieces), *qkv_near))
    out_full = far_join(*out_near)
    cot_half = my_half(cotangent)
    cot_near = send(after(cot_half, *out_near), "first")
    down_pair = ffn_pair([after(w_down, *out_near)])

    segment, position = layout(lengths[0])
    cosine, sine_table = angles(position)
    sign = jnp.where(jnp.arange(HD) < HD // 2, -1.0, 1.0)
    signed_sine = sine_table * sign
    start = (jnp.arange(SEQ, dtype=jnp.int32) - position)[:, None]
    stream = inputs.astype(f32)
    inv_one = lax.rsqrt(jnp.mean(stream * stream, axis=-1, keepdims=True) + EPSILON)
    qkv_full = after(qkv_full, cosine, signed_sine, start, inv_one)
    gain_one = qkv_full[:, qkv_cols].astype(f32)
    gain_two = qkv_full[:, qkv_cols + 1].astype(f32)
    qkv_full = qkv_full[:, :qkv_cols]

    h_one = (stream * inv_one * gain_one).astype(bf16)
    qkv_bias = jnp.concatenate([b_query, b_key, b_value]).astype(f32)
    qkv_pre = plain_dot(h_one, qkv_full) + qkv_bias
    q_rot, k_rot, v_low, attended, lse = attend(qkv_pre, cosine, signed_sine, start)
    branch = trans_dot(attended, out_full)
    resid = (
        my_half(stream)
        + my_half(branch)
        + send(other_half(branch).astype(bf16), "t").astype(f32)
    )
    inv_two = lax.rsqrt(jnp.mean(resid * resid, axis=-1, keepdims=True) + EPSILON)
    norm_two = resid * inv_two
    h_two_half = after((norm_two * gain_two).astype(bf16), down_pair)
    h_two, h_two_far = square_far(h_two_half, send(h_two_half, "first"))
    cot_all, _ = square_far(cot_half, cot_near, h_two_far)
    down_full = ffn_gather(after(down_pair, gate_up_pair))

    gate_full = gate_up_full[:, :quarter]
    up_full = gate_up_full[:, quarter:]
    gate_low = plain_dot(h_two, gate_full).astype(bf16)
    up_low = plain_dot(h_two, up_full).astype(bf16)
    gate_pre = gate_low.astype(f32)
    up_pre = up_low.astype(f32)
    sigmoid_gate = jax.nn.sigmoid(gate_pre)
    swish_gate = gate_pre * sigmoid_gate
    hidden = (swish_gate * up_pre).astype(bf16)
    down_part = outer_dot(cot_all, hidden).astype(bf16)
    down_sum = ffn_scatter(down_part)
    d_hidden = plain_dot(after(cot_all, down_part), down_full)
    d_gate = (d_hidden * up_pre * sigmoid_gate * (1.0 + gate_pre * (1.0 - sigmoid_gate))).astype(
        bf16
    )
    d_up = (d_hidden * swish_gate).astype(bf16)
    mid = 4 * half

    def entry(gate_side, up_side):
        return (trans_dot(gate_side, gate_full) + trans_dot(up_side, up_full)).astype(bf16)

    theirs = entry(d_gate[mid:], d_up[mid:])
    mine = entry(after(d_gate[:mid], theirs), d_up[:mid])
    d_h_two = square_scatter(mine, theirs)
    gate_part = outer_dot(after(h_two, mine), d_gate).astype(bf16)
    gate_sum = ffn_scatter(gate_part)
    up_part = outer_dot(after(h_two, gate_part), d_up).astype(bf16)
    up_sum = ffn_scatter(up_part)
    low_hidden = after(hidden, up_part)
    ffn_theirs = trans_dot(low_hidden[mid:], down_full).astype(bf16)
    ffn_mine = trans_dot(low_hidden[:mid], down_full).astype(bf16)

    scaled = d_h_two * gain_two
    d_resid = cot_half.astype(f32) + inv_two * (
        scaled - norm_two * jnp.mean(norm_two * scaled, axis=-1, keepdims=True)
    )
    gain_two_part = jnp.sum(d_h_two * norm_two, axis=0)
    d_out_low = both_halves(d_resid.astype(bf16))
    out_grad, _, _ = attn_scatter(outer_dot(d_out_low, attended).astype(bf16))
    ffn_total = square_scatter(ffn_mine, ffn_theirs, d_out_low)
    layer_out = both_halves((resid + ffn_total).astype(bf16))
    d_attended = plain_dot(d_out_low, out_full).astype(bf16)
    d_qkv = attend_back(q_rot, k_rot, v_low, d_attended, lse, cosine, signed_sine, start)
    qkv_grad, qkv_blocks, qkv_mine = attn_scatter(outer_dot(h_one, d_qkv).astype(bf16))
    down_grad = ffn_swap(after(down_sum, d_out_low))
    gate_grad = ffn_swap(after(gate_sum, qkv_blocks))
    up_grad = ffn_swap(after(up_sum, qkv_mine))
    entry_one = trans_dot(d_qkv, qkv_full)
    d_h_one = my_half(entry_one) + send(other_half(entry_one).astype(bf16), "t").astype(f32)
    half_inv = my_half(inv_one)
    norm_one = my_half(stream) * half_inv
    scaled = d_h_one * gain_one
    input_grad = both_halves(
        (
            d_resid
            + half_inv * (scaled - norm_one * jnp.mean(norm_one * scaled, axis=-1, keepdims=True))
        ).astype(bf16)
    )
    gain_one_part = jnp.sum(d_h_one * norm_one, axis=0)

    bias_part = jnp.sum(d_qkv.astype(f32), axis=0)
    small = jnp.concatenate([gain_one_part, gain_two_part, bias_part]).reshape(-1, 128)
    small = small + send(small, "y")
    step = 1
    while step < dp_count:
        small = small + lax.ppermute(small, "dp", [(i, i ^ step) for i in range(dp_count)])
        step *= 2
    small = small.reshape(-1)
    gain_sums = small[: 2 * d_model].reshape(2, dp_count, rows)
    gain_mine = lax.dynamic_index_in_dim(gain_sums, dp_index, 1, keepdims=False)
    gain_mine = gain_mine + send(gain_mine, "t")
    bias_sum = small[2 * d_model :]
    return (
        layer_out,
        input_grad,
        gain_mine[0],
        qkv_grad[:, :query_cols],
        bias_sum[:query_cols],
        qkv_grad[:, query_cols : query_cols + key_cols],
        bias_sum[query_cols : query_cols + key_cols],
        qkv_grad[:, query_cols + key_cols :],
        bias_sum[query_cols + key_cols :],
        out_grad,
        gain_mine[1],
        gate_grad,
        up_grad,
        down_grad,
    )


def solution(mesh):
    in_specs = (
        P(("group", "dp"), None),
        P(("group", "dp"), None),
        P(("group", "dp"), None),
        P("dp"),
        P("dp", "tensor"),
        P("tensor"),
        P("dp", "tensor"),
        P("tensor"),
        P("dp", "tensor"),
        P("tensor"),
        P("dp", "tensor"),
        P("dp"),
        P("dp", "tensor"),
        P("dp", "tensor"),
        P("dp", "tensor"),
    )
    out_specs = (
        P(("group", "dp"), None),
        P(("group", "dp"), None),
        P("dp"),
        P("dp", "tensor"),
        P("tensor"),
        P("dp", "tensor"),
        P("tensor"),
        P("dp", "tensor"),
        P("tensor"),
        P("dp", "tensor"),
        P("dp"),
        P("dp", "tensor"),
        P("dp", "tensor"),
        P("dp", "tensor"),
    )
    return jax.shard_map(local, mesh=mesh, in_specs=in_specs, out_specs=out_specs, check_vma=False)
```

```python
import math

import jax
import jax.numpy as jnp
from jax import lax
from jax.experimental import pallas as pl
from jax.experimental.pallas import tpu as pltpu
from jax.sharding import PartitionSpec as P

HD = 128
SEQ = 768
NSEG = 3


EPSILON = 1e-06
THETA = 10000.0
MASKED_SCORE = -1e30


def layout(lengths):
    segment_ends = jnp.cumsum(lengths, axis=-1)
    segment_starts = segment_ends - lengths
    places = jnp.arange(SEQ, dtype=jnp.int32)
    segment = jnp.sum((places[:, None] >= segment_ends[..., None, :]).astype(jnp.int32), axis=-1)
    choose = segment[..., None] == jnp.arange(NSEG, dtype=jnp.int32)
    picked = jnp.sum(jnp.where(choose, segment_starts[..., None, :], 0), axis=-1)
    return (segment, places - picked)


def angles(position):
    frequency = jnp.exp(-(math.log(THETA) * 2.0 / HD) * jnp.arange(HD // 2, dtype=jnp.float32))
    phase_angle = position.astype(jnp.float32)[..., None] * frequency
    phase_angle = jnp.concatenate([phase_angle, phase_angle], axis=-1)
    return (jnp.cos(phase_angle), jnp.sin(phase_angle))


def plain_dot(left_side, right_side):
    return jnp.dot(left_side, right_side, preferred_element_type=jnp.float32)


def trans_dot(left_side, right_side):
    return lax.dot_general(
        left_side, right_side, (((1,), (1,)), ((), ())), preferred_element_type=jnp.float32
    )


def outer_dot(left_side, right_side):
    return lax.dot_general(
        left_side, right_side, (((0,), (0,)), ((), ())), preferred_element_type=jnp.float32
    )


BLOCK = 256


def rotated(values, cosine, signed_sine):
    return values * cosine + pltpu.roll(values, HD // 2, 1) * signed_sine


def unrotated(values, cosine, signed_sine):
    return values * cosine - pltpu.roll(values, HD // 2, 1) * signed_sine


def allowed_block(start, top, width):
    row = top + lax.broadcasted_iota(jnp.int32, (BLOCK, width), 0)
    col = lax.broadcasted_iota(jnp.int32, (BLOCK, width), 1)
    return (col >= start) & (col <= row)


def attend_body(
    q_pre, k_pre, v_pre, cosine, signed_sine, start, q_out, k_out, v_out, att_out, lse_out
):
    head = pl.program_id(0)

    @pl.when(head == 0)
    def _():
        k_out[...] = rotated(k_pre[...], cosine[...], signed_sine[...]).astype(jnp.bfloat16)
        v_out[...] = v_pre[...].astype(jnp.bfloat16)
        lse_out[...] = jnp.zeros_like(lse_out)

    q_out[...] = rotated(q_pre[...], cosine[...], signed_sine[...]).astype(jnp.bfloat16)
    for top in range(0, SEQ, BLOCK):
        width = top + BLOCK
        rows = pl.ds(top, BLOCK)
        scores = trans_dot(q_out[rows, :], k_out[:width, :]) * HD ** (-0.5)
        scores = jnp.where(allowed_block(start[rows, :], top, width), scores, MASKED_SCORE)
        row_max = jnp.max(scores, axis=1, keepdims=True)
        terms = jnp.exp(scores - row_max)
        total = jnp.sum(terms, axis=1, keepdims=True)
        probs = (terms * (1.0 / total)).astype(jnp.bfloat16)
        att_out[rows, :] = plain_dot(probs, v_out[:width, :]).astype(jnp.bfloat16)
        lane = lax.broadcasted_iota(jnp.int32, (BLOCK, HD), 1)
        lse_out[rows, :] = jnp.where(lane == head, row_max + jnp.log(total), lse_out[rows, :])


def attend_back_body(
    q_rot, k_rot, v_low, d_att, lse, cosine, signed_sine, start, grad_out, dk_sum, dv_sum
):
    head = pl.program_id(0)

    @pl.when(head == 0)
    def _():
        dk_sum[...] = jnp.zeros_like(dk_sum)
        dv_sum[...] = jnp.zeros_like(dv_sum)

    for top in range(0, SEQ, BLOCK):
        width = top + BLOCK
        rows = pl.ds(top, BLOCK)
        query = q_rot[rows, :]
        d_out = d_att[rows, :]
        lane = lax.broadcasted_iota(jnp.int32, (BLOCK, HD), 1)
        row_lse = jnp.sum(jnp.where(lane == head, lse[rows, :], 0.0), axis=1, keepdims=True)
        scores = trans_dot(query, k_rot[:width, :]) * HD ** (-0.5)
        scores = jnp.where(allowed_block(start[rows, :], top, width), scores, MASKED_SCORE)
        probs = jnp.exp(scores - row_lse)
        d_probs = trans_dot(d_out, v_low[:width, :])
        inner = jnp.sum(probs * d_probs, axis=1, keepdims=True)
        d_scores = (probs * (d_probs - inner)).astype(jnp.bfloat16)
        d_query = plain_dot(d_scores, k_rot[:width, :]) * HD ** (-0.5)
        d_query = unrotated(d_query, cosine[rows, :], signed_sine[rows, :])
        cols = pl.ds(pl.multiple_of(head * HD, HD), HD)
        grad_out[rows, cols] = d_query.astype(jnp.bfloat16)
        dk_sum[:width, :] += outer_dot(d_scores, query)
        dv_sum[:width, :] += outer_dot(probs.astype(jnp.bfloat16), d_out)

    @pl.when(head == pl.num_programs(0) - 1)
    def _():
        edge = grad_out.shape[1] - 2 * HD
        d_key = unrotated(dk_sum[...] * HD ** (-0.5), cosine[...], signed_sine[...])
        grad_out[:, edge : edge + HD] = d_key.astype(jnp.bfloat16)
        grad_out[:, edge + HD :] = dv_sum[...].astype(jnp.bfloat16)


def fixed(shape):
    return pl.BlockSpec(shape, lambda head: (0, 0))


def column(index):
    return pl.BlockSpec((SEQ, HD), lambda head: (0, index))


PER_HEAD = pl.BlockSpec((SEQ, HD), lambda head: (0, head))
WHOLE = (SEQ, HD)


def attend(qkv_pre, cosine, signed_sine, start):
    heads = qkv_pre.shape[1] // HD - 2
    shape = lambda cols, kind: jax.ShapeDtypeStruct((SEQ, cols), kind)
    low = jnp.bfloat16
    return pl.pallas_call(
        attend_body,
        grid=(heads,),
        in_specs=[PER_HEAD, column(heads), column(heads + 1)]
        + [fixed(WHOLE), fixed(WHOLE), fixed((SEQ, 1))],
        out_specs=[PER_HEAD, fixed(WHOLE), fixed(WHOLE), PER_HEAD, fixed(WHOLE)],
        out_shape=[
            shape(heads * HD, low),
            shape(HD, low),
            shape(HD, low),
            shape(heads * HD, low),
            shape(HD, jnp.float32),
        ],
    )(qkv_pre, qkv_pre, qkv_pre, cosine, signed_sine, start)


def attend_back(q_rot, k_rot, v_low, d_att, lse, cosine, signed_sine, start):
    heads = q_rot.shape[1] // HD
    cols = (heads + 2) * HD
    return pl.pallas_call(
        attend_back_body,
        grid=(heads,),
        in_specs=[PER_HEAD, fixed(WHOLE), fixed(WHOLE), PER_HEAD, fixed(WHOLE)]
        + [fixed(WHOLE), fixed(WHOLE), fixed((SEQ, 1))],
        out_specs=fixed((SEQ, cols)),
        out_shape=jax.ShapeDtypeStruct((SEQ, cols), jnp.bfloat16),
        scratch_shapes=[pltpu.VMEM(WHOLE, jnp.float32), pltpu.VMEM(WHOLE, jnp.float32)],
    )(q_rot, k_rot, v_low, d_att, lse, cosine, signed_sine, start)


AXES = ("group", "dp", "tensor")


def routes(dp_count):
    def table(move):
        flat = lambda g, d, t: (g * dp_count + d) * 2 + t
        return [
            (flat(g, d, t), flat(*move(g, d, t)))
            for g in range(2)
            for d in range(dp_count)
            for t in range(2)
        ]

    shifts = {
        step: table(lambda g, d, t: (g, (d + 2 * step) % dp_count, t))
        for step in range(1, dp_count // 2)
    }
    return shifts | {
        "x": table(lambda g, d, t: (g, d ^ 1, t)),
        "y": table(lambda g, d, t: (g ^ 1, d, t)),
        "t": table(lambda g, d, t: (g, d, t ^ 1)),
        "first": table(lambda g, d, t: (g, d ^ 1, t) if t == 0 else (g ^ 1, d, t)),
        "second": table(lambda g, d, t: (g ^ 1, d, t) if t == 0 else (g, d ^ 1, t)),
    }


def local(
    inputs,
    cotangent,
    lengths,
    attn_gain,
    w_query,
    b_query,
    w_key,
    b_key,
    w_value,
    b_value,
    w_out,
    ffn_gain,
    w_gate,
    w_up,
    w_down,
):
    bf16 = jnp.bfloat16
    f32 = jnp.float32
    dp_count = lax.axis_size("dp")
    line = dp_count // 2
    dp_index = lax.axis_index("dp")
    x_index = dp_index % 2
    z_index = dp_index // 2
    y_index = lax.axis_index("group")
    core = lax.axis_index("tensor")
    table = routes(dp_count)
    line_groups = [[2 * z + x for z in range(line)] for x in range(2)]
    tokens, d_model = inputs.shape
    half = tokens // 2
    rows = w_query.shape[0]
    head_count = w_query.shape[1] // HD
    kv_count = w_key.shape[1] // HD
    ffn_cols = w_gate.shape[1]
    quarter = -(-ffn_cols // 512) * 128

    def send(value, route):
        return lax.ppermute(value, AXES, table[route])

    def pick(value, index):
        return lax.dynamic_index_in_dim(value, index, 0, keepdims=False)

    def in_order(index, mine, other):
        first = index == 0
        return jnp.where(first, mine, other), jnp.where(first, other, mine)

    def my_half(value):
        return pick(value.reshape(2, half, value.shape[-1]), core)

    def other_half(value):
        return pick(value.reshape(2, half, value.shape[-1]), 1 - core)

    def both_halves(mine):
        return jnp.concatenate(in_order(core, mine, send(mine, "t")), axis=0)

    def after(value, *others):
        return lax.optimization_barrier((value, *others))[0]

    def square_far(mine, near, *others):
        mine_sib = send(mine, "t")
        near_sib = send(near, "t")
        far = send(after(jnp.stack([mine, near]), *others), "second")
        far_sib = send(far, "t")
        whole = jnp.concatenate(
            [mine, near, far[0], far[1], mine_sib, near_sib, far_sib[0], far_sib[1]], axis=0
        )
        return whole, far

    def scatter_far(mine, theirs):
        came = send(theirs, "t")
        total = (mine.astype(f32) + came.astype(f32)).reshape(4, half, d_model)
        return total[:2], send(total[2:].astype(bf16), "second")

    def scatter_near(kept, came):
        total = kept + came.astype(f32)
        came = send(total[1].astype(bf16), "first")
        return total[0] + came.astype(f32)

    def ffn_quarter(weight, index):
        parts = [weight[:, i * quarter : (i + 1) * quarter] for i in range(4)]
        parts[3] = jnp.pad(parts[3], ((0, 0), (0, 4 * quarter - ffn_cols)))
        upper = jnp.where(index % 2 == 0, parts[2], parts[3])
        lower = jnp.where(index % 2 == 0, parts[0], parts[1])
        return jnp.where(index < 2, lower, upper)

    def ffn_pair(weights):
        other = [ffn_quarter(w, (1 - x_index) * 2 + y_index) for w in weights]
        came = send(jnp.concatenate(other, axis=1), "x")
        mine = [ffn_quarter(w, x_index * 2 + y_index) for w in weights]
        return jnp.stack(in_order(x_index, jnp.concatenate(mine, axis=1), came))

    def ffn_gather(pair):
        full = lax.all_gather(pair, "dp", axis=0, axis_index_groups=line_groups)
        return full.reshape(d_model, pair.shape[-1])

    def ffn_scatter(grad):
        parts = grad.astype(bf16).reshape(line, 2 * rows, quarter)
        return lax.psum_scatter(
            parts, "dp", scatter_dimension=0, axis_index_groups=line_groups
        ).reshape(2, rows, quarter)

    def ffn_swap(summed):
        came = send(pick(summed, 1 - x_index), "x")
        pair = jnp.stack(in_order(x_index, pick(summed, x_index), came))
        low, high = in_order(y_index, pair, send(pair, "y"))
        whole = jnp.concatenate([low[0], high[0], low[1], high[1]], axis=1)
        return whole[:, :ffn_cols].astype(f32)

    cut = line // 2
    part_rows = rows // 2

    def line_sends(weight):
        mine = lax.dynamic_slice_in_dim(weight, y_index * part_rows, part_rows, 0)
        return [mine] + [send(mine, step) for step in range(1, line)]

    def line_join(pieces):
        whole = jnp.zeros((line,) + pieces[0].shape, bf16)
        for step, piece in enumerate(pieces):
            spot = ((z_index - step) % line, 0, 0)
            whole = lax.dynamic_update_slice(whole, piece[None], spot)
        return whole

    def near_sends(blocks):
        low, high = blocks[:cut], blocks[cut:]
        return low, high, send(low, "x"), send(high, "y")

    def far_join(low, high, low_near, high_near):
        low_far = send(jnp.stack([low, low_near]), "y")
        high_far = send(jnp.stack([high, high_near]), "x")
        cols = low.shape[-1]
        whole = jnp.zeros((line, 2, 2, part_rows, cols), bf16)
        x, y = x_index, y_index
        for piece, z, px, py in (
            (low, 0, x, y),
            (low_near, 0, 1 - x, y),
            (low_far[0], 0, x, 1 - y),
            (low_far[1], 0, 1 - x, 1 - y),
            (high, cut, x, y),
            (high_near, cut, x, 1 - y),
            (high_far[0], cut, 1 - x, y),
            (high_far[1], cut, 1 - x, 1 - y),
        ):
            whole = lax.dynamic_update_slice(whole, piece[:, None, None], (z, px, py, 0, 0))
        return whole.reshape(d_model, cols)

    def take(value, axis, index):
        return lax.dynamic_index_in_dim(value, index, axis, keepdims=False)

    def fold(value, axis, index, route):
        came = send(take(value, axis, 1 - index), route)
        return (take(value, axis, index).astype(f32) + came.astype(f32)).astype(bf16)

    def scatter_hop1(grad):
        view = grad.reshape(line, 2, 2, part_rows, grad.shape[-1])
        return fold(view[:cut], 1, x_index, "x"), fold(view[cut:], 2, y_index, "y")

    def scatter_hop2(low, high):
        return jnp.concatenate([fold(low, 1, y_index, "y"), fold(high, 1, x_index, "x")])

    def scatter_line(blocks):
        total = pick(blocks, z_index).astype(f32)
        for step in range(1, line):
            total = total + send(pick(blocks, (z_index + step) % line), step).astype(f32)
        return total.astype(bf16)

    def scatter_end(mine):
        return jnp.concatenate(in_order(y_index, mine, send(mine, "y"))).astype(f32)

    query_cols = head_count * HD
    key_cols = kv_count * HD
    qkv_cols = query_cols + 2 * key_cols
    gains = jnp.pad(jnp.stack([attn_gain, ffn_gain], axis=1), ((0, 0), (0, HD - 2)))

    qkv_pieces = line_sends(jnp.concatenate([w_query, w_key, w_value, gains], axis=1))
    down_pair = ffn_pair([w_down])
    gate_up_pair = ffn_pair([after(w_gate, down_pair), w_up])
    down_full = ffn_gather(down_pair)
    gate_up_full = ffn_gather(gate_up_pair)
    qkv_near = near_sends(after(line_join(qkv_pieces), down_pair, gate_up_pair))
    qkv_full = far_join(*qkv_near)
    out_pieces = line_sends(after(w_out, *qkv_near))
    out_near = near_sends(after(line_join(out_pieces), qkv_full))
    out_full = far_join(*out_near)
    cot_half = my_half(cotangent)
    cot_near = send(after(cot_half, *out_near), "first")

    segment, position = layout(lengths[0])
    cosine, sine_table = angles(position)
    sign = jnp.where(jnp.arange(HD) < HD // 2, -1.0, 1.0)
    signed_sine = sine_table * sign
    start = (jnp.arange(SEQ, dtype=jnp.int32) - position)[:, None]
    stream = inputs.astype(f32)
    inv_one = lax.rsqrt(jnp.mean(stream * stream, axis=-1, keepdims=True) + EPSILON)
    qkv_full = after(qkv_full, cosine, signed_sine, start, inv_one)
    gain_one = qkv_full[:, qkv_cols].astype(f32)
    gain_two = qkv_full[:, qkv_cols + 1].astype(f32)
    qkv_full = qkv_full[:, :qkv_cols]

    h_one = (stream * inv_one * gain_one).astype(bf16)
    qkv_bias = jnp.concatenate([b_query, b_key, b_value]).astype(f32)
    qkv_pre = plain_dot(h_one, qkv_full) + qkv_bias
    q_rot, k_rot, v_low, attended, lse = attend(
        after(qkv_pre, *out_near), cosine, signed_sine, start
    )
    branch = trans_dot(attended, out_full)
    resid = (
        my_half(stream)
        + my_half(branch)
        + send(other_half(branch).astype(bf16), "t").astype(f32)
    )
    inv_two = lax.rsqrt(jnp.mean(resid * resid, axis=-1, keepdims=True) + EPSILON)
    norm_two = resid * inv_two
    h_two_half = after((norm_two * gain_two).astype(bf16), cot_near)
    h_two, h_two_far = square_far(h_two_half, send(h_two_half, "first"))
    cot_all, _ = square_far(cot_half, cot_near, h_two_far)
    d_hidden = after(plain_dot(cot_all, down_full).astype(bf16), cot_near)
    h_two = after(h_two, d_hidden)

    gate_full = gate_up_full[:, :quarter]
    up_full = gate_up_full[:, quarter:]
    gate_low = plain_dot(h_two, gate_full).astype(bf16)
    up_low = plain_dot(after(h_two, gate_low), up_full).astype(bf16)
    gate_pre = gate_low.astype(f32)
    up_pre = up_low.astype(f32)
    d_hid = d_hidden.astype(f32)
    sigmoid_gate = jax.nn.sigmoid(gate_pre)
    swish_gate = gate_pre * sigmoid_gate
    hidden = (swish_gate * up_pre).astype(bf16)
    d_gate = (d_hid * up_pre * sigmoid_gate * (1.0 + gate_pre * (1.0 - sigmoid_gate))).astype(bf16)
    d_up = (d_hid * swish_gate).astype(bf16)
    mid = 4 * half
    down_part = outer_dot(cot_all, hidden).astype(bf16)
    down_sum = ffn_scatter(down_part)
    low_hidden = after(hidden, down_part)
    ffn_theirs = trans_dot(low_hidden[mid:], down_full).astype(bf16)
    ffn_mine = trans_dot(after(low_hidden[:mid], ffn_theirs), down_full).astype(bf16)
    ffn_kept, ffn_came = scatter_far(ffn_mine, ffn_theirs)

    def entry(gate_side, up_side):
        return (trans_dot(gate_side, gate_full) + trans_dot(up_side, up_full)).astype(bf16)

    theirs = entry(after(d_gate[mid:], ffn_mine), d_up[mid:])
    mine = entry(after(d_gate[:mid], theirs), d_up[:mid])
    ffn_total = scatter_near(ffn_kept, after(ffn_came, theirs))
    kept, came = scatter_far(after(mine, ffn_came), theirs)
    gate_part = outer_dot(after(h_two, mine, ffn_total), d_gate).astype(bf16)
    gate_sum = ffn_scatter(gate_part)
    d_h_two = scatter_near(kept, after(came, gate_part))
    up_part = outer_dot(after(h_two, gate_part), d_up).astype(bf16)
    up_sum = ffn_scatter(up_part)
    layer_out = both_halves((resid + ffn_total).astype(bf16))

    scaled = d_h_two * gain_two
    d_resid = cot_half.astype(f32) + inv_two * (
        scaled - norm_two * jnp.mean(norm_two * scaled, axis=-1, keepdims=True)
    )
    gain_two_part = jnp.sum(d_h_two * norm_two, axis=0)
    d_out_low = both_halves(d_resid.astype(bf16))
    out_hop = scatter_hop1(outer_dot(d_out_low, attended).astype(bf16))
    down_grad = ffn_swap(after(down_sum, came))
    d_attended = plain_dot(d_out_low, out_full).astype(bf16)
    d_attended = after(d_attended, down_sum)
    d_qkv = attend_back(q_rot, k_rot, v_low, d_attended, lse, cosine, signed_sine, start)
    qkv_part = outer_dot(after(h_one, *out_hop, down_grad), d_qkv).astype(bf16)
    out_mine = scatter_line(scatter_hop2(*out_hop))
    qkv_blocks = scatter_hop2(*scatter_hop1(qkv_part))
    qkv_mine = scatter_line(after(qkv_blocks, out_mine))
    out_grad = scatter_end(out_mine)
    qkv_grad = scatter_end(qkv_mine)
    gate_grad = ffn_swap(after(gate_sum, qkv_blocks))
    entry_one = trans_dot(d_qkv, qkv_full)
    d_h_one = my_half(entry_one) + send(other_half(entry_one).astype(bf16), "t").astype(f32)
    half_inv = my_half(inv_one)
    norm_one = my_half(stream) * half_inv
    scaled = d_h_one * gain_one
    input_grad = both_halves(
        (
            d_resid
            + half_inv * (scaled - norm_one * jnp.mean(norm_one * scaled, axis=-1, keepdims=True))
        ).astype(bf16)
    )
    gain_one_part = jnp.sum(d_h_one * norm_one, axis=0)

    bias_part = jnp.sum(d_qkv.astype(f32), axis=0)
    small = jnp.concatenate([gain_one_part, gain_two_part, bias_part]).reshape(-1, 128)
    small = small + send(small, "y")
    step = 1
    while step < dp_count:
        small = small + lax.ppermute(small, "dp", [(i, i ^ step) for i in range(dp_count)])
        step *= 2
    small = small.reshape(-1)
    up_grad = ffn_swap(after(up_sum, gate_grad, qkv_mine, small))
    gain_sums = small[: 2 * d_model].reshape(2, dp_count, rows)
    gain_mine = lax.dynamic_index_in_dim(gain_sums, dp_index, 1, keepdims=False)
    gain_mine = gain_mine + send(gain_mine, "t")
    bias_sum = small[2 * d_model :]
    return (
        layer_out,
        input_grad,
        gain_mine[0],
        qkv_grad[:, :query_cols],
        bias_sum[:query_cols],
        qkv_grad[:, query_cols : query_cols + key_cols],
        bias_sum[query_cols : query_cols + key_cols],
        qkv_grad[:, query_cols + key_cols :],
        bias_sum[query_cols + key_cols :],
        out_grad,
        gain_mine[1],
        gate_grad,
        up_grad,
        down_grad,
    )


def solution(mesh):
    in_specs = (
        P(("group", "dp"), None),
        P(("group", "dp"), None),
        P(("group", "dp"), None),
        P("dp"),
        P("dp", "tensor"),
        P("tensor"),
        P("dp", "tensor"),
        P("tensor"),
        P("dp", "tensor"),
        P("tensor"),
        P("dp", "tensor"),
        P("dp"),
        P("dp", "tensor"),
        P("dp", "tensor"),
        P("dp", "tensor"),
    )
    out_specs = (
        P(("group", "dp"), None),
        P(("group", "dp"), None),
        P("dp"),
        P("dp", "tensor"),
        P("tensor"),
        P("dp", "tensor"),
        P("tensor"),
        P("dp", "tensor"),
        P("tensor"),
        P("dp", "tensor"),
        P("dp"),
        P("dp", "tensor"),
        P("dp", "tensor"),
        P("dp", "tensor"),
    )
    return jax.shard_map(local, mesh=mesh, in_specs=in_specs, out_specs=out_specs, check_vma=False)
```

```python
import math

import jax
import jax.numpy as jnp
from jax import lax
from jax.experimental import pallas as pl
from jax.experimental.pallas import tpu as pltpu
from jax.sharding import PartitionSpec as P

HD = 128
SEQ = 768
NSEG = 3


EPSILON = 1e-06
THETA = 10000.0
MASKED_SCORE = -1e30


def layout(lengths):
    segment_ends = jnp.cumsum(lengths, axis=-1)
    segment_starts = segment_ends - lengths
    places = jnp.arange(SEQ, dtype=jnp.int32)
    segment = jnp.sum((places[:, None] >= segment_ends[..., None, :]).astype(jnp.int32), axis=-1)
    choose = segment[..., None] == jnp.arange(NSEG, dtype=jnp.int32)
    picked = jnp.sum(jnp.where(choose, segment_starts[..., None, :], 0), axis=-1)
    return (segment, places - picked)


def angles(position):
    frequency = jnp.exp(-(math.log(THETA) * 2.0 / HD) * jnp.arange(HD // 2, dtype=jnp.float32))
    phase_angle = position.astype(jnp.float32)[..., None] * frequency
    phase_angle = jnp.concatenate([phase_angle, phase_angle], axis=-1)
    return (jnp.cos(phase_angle), jnp.sin(phase_angle))


def plain_dot(left_side, right_side):
    return jnp.dot(left_side, right_side, preferred_element_type=jnp.float32)


def trans_dot(left_side, right_side):
    return lax.dot_general(
        left_side, right_side, (((1,), (1,)), ((), ())), preferred_element_type=jnp.float32
    )


def outer_dot(left_side, right_side):
    return lax.dot_general(
        left_side, right_side, (((0,), (0,)), ((), ())), preferred_element_type=jnp.float32
    )


BLOCK = 256


def rotated(values, cosine, signed_sine):
    return values * cosine + pltpu.roll(values, HD // 2, 1) * signed_sine


def unrotated(values, cosine, signed_sine):
    return values * cosine - pltpu.roll(values, HD // 2, 1) * signed_sine


def allowed_block(start, top, width):
    row = top + lax.broadcasted_iota(jnp.int32, (BLOCK, width), 0)
    col = lax.broadcasted_iota(jnp.int32, (BLOCK, width), 1)
    return (col >= start) & (col <= row)


def attend_body(
    q_pre, k_pre, v_pre, cosine, signed_sine, start, q_out, k_out, v_out, att_out, lse_out
):
    head = pl.program_id(0)

    @pl.when(head == 0)
    def _():
        k_out[...] = rotated(k_pre[...], cosine[...], signed_sine[...]).astype(jnp.bfloat16)
        v_out[...] = v_pre[...].astype(jnp.bfloat16)
        lse_out[...] = jnp.zeros_like(lse_out)

    q_out[...] = rotated(q_pre[...], cosine[...], signed_sine[...]).astype(jnp.bfloat16)
    for top in range(0, SEQ, BLOCK):
        width = top + BLOCK
        rows = pl.ds(top, BLOCK)
        scores = trans_dot(q_out[rows, :], k_out[:width, :]) * HD ** (-0.5)
        scores = jnp.where(allowed_block(start[rows, :], top, width), scores, MASKED_SCORE)
        row_max = jnp.max(scores, axis=1, keepdims=True)
        terms = jnp.exp(scores - row_max)
        total = jnp.sum(terms, axis=1, keepdims=True)
        probs = (terms * (1.0 / total)).astype(jnp.bfloat16)
        att_out[rows, :] = plain_dot(probs, v_out[:width, :]).astype(jnp.bfloat16)
        lane = lax.broadcasted_iota(jnp.int32, (BLOCK, HD), 1)
        lse_out[rows, :] = jnp.where(lane == head, row_max + jnp.log(total), lse_out[rows, :])


def attend_back_body(
    q_rot, k_rot, v_low, d_att, lse, cosine, signed_sine, start, grad_out, dk_sum, dv_sum
):
    head = pl.program_id(0)

    @pl.when(head == 0)
    def _():
        dk_sum[...] = jnp.zeros_like(dk_sum)
        dv_sum[...] = jnp.zeros_like(dv_sum)

    for top in range(0, SEQ, BLOCK):
        width = top + BLOCK
        rows = pl.ds(top, BLOCK)
        query = q_rot[rows, :]
        d_out = d_att[rows, :]
        lane = lax.broadcasted_iota(jnp.int32, (BLOCK, HD), 1)
        row_lse = jnp.sum(jnp.where(lane == head, lse[rows, :], 0.0), axis=1, keepdims=True)
        scores = trans_dot(query, k_rot[:width, :]) * HD ** (-0.5)
        scores = jnp.where(allowed_block(start[rows, :], top, width), scores, MASKED_SCORE)
        probs = jnp.exp(scores - row_lse)
        d_probs = trans_dot(d_out, v_low[:width, :])
        inner = jnp.sum(probs * d_probs, axis=1, keepdims=True)
        d_scores = (probs * (d_probs - inner)).astype(jnp.bfloat16)
        d_query = plain_dot(d_scores, k_rot[:width, :]) * HD ** (-0.5)
        d_query = unrotated(d_query, cosine[rows, :], signed_sine[rows, :])
        cols = pl.ds(pl.multiple_of(head * HD, HD), HD)
        grad_out[rows, cols] = d_query.astype(jnp.bfloat16)
        dk_sum[:width, :] += outer_dot(d_scores, query)
        dv_sum[:width, :] += outer_dot(probs.astype(jnp.bfloat16), d_out)

    @pl.when(head == pl.num_programs(0) - 1)
    def _():
        edge = grad_out.shape[1] - 2 * HD
        d_key = unrotated(dk_sum[...] * HD ** (-0.5), cosine[...], signed_sine[...])
        grad_out[:, edge : edge + HD] = d_key.astype(jnp.bfloat16)
        grad_out[:, edge + HD :] = dv_sum[...].astype(jnp.bfloat16)


def fixed(shape):
    return pl.BlockSpec(shape, lambda head: (0, 0))


def column(index):
    return pl.BlockSpec((SEQ, HD), lambda head: (0, index))


PER_HEAD = pl.BlockSpec((SEQ, HD), lambda head: (0, head))
WHOLE = (SEQ, HD)


def attend(qkv_pre, cosine, signed_sine, start):
    heads = qkv_pre.shape[1] // HD - 2
    shape = lambda cols, kind: jax.ShapeDtypeStruct((SEQ, cols), kind)
    low = jnp.bfloat16
    return pl.pallas_call(
        attend_body,
        grid=(heads,),
        in_specs=[PER_HEAD, column(heads), column(heads + 1)]
        + [fixed(WHOLE), fixed(WHOLE), fixed((SEQ, 1))],
        out_specs=[PER_HEAD, fixed(WHOLE), fixed(WHOLE), PER_HEAD, fixed(WHOLE)],
        out_shape=[
            shape(heads * HD, low),
            shape(HD, low),
            shape(HD, low),
            shape(heads * HD, low),
            shape(HD, jnp.float32),
        ],
    )(qkv_pre, qkv_pre, qkv_pre, cosine, signed_sine, start)


def attend_back(q_rot, k_rot, v_low, d_att, lse, cosine, signed_sine, start):
    heads = q_rot.shape[1] // HD
    cols = (heads + 2) * HD
    return pl.pallas_call(
        attend_back_body,
        grid=(heads,),
        in_specs=[PER_HEAD, fixed(WHOLE), fixed(WHOLE), PER_HEAD, fixed(WHOLE)]
        + [fixed(WHOLE), fixed(WHOLE), fixed((SEQ, 1))],
        out_specs=fixed((SEQ, cols)),
        out_shape=jax.ShapeDtypeStruct((SEQ, cols), jnp.bfloat16),
        scratch_shapes=[pltpu.VMEM(WHOLE, jnp.float32), pltpu.VMEM(WHOLE, jnp.float32)],
    )(q_rot, k_rot, v_low, d_att, lse, cosine, signed_sine, start)


AXES = ("group", "dp", "tensor")


def routes(dp_count):
    def table(move):
        flat = lambda g, d, t: (g * dp_count + d) * 2 + t
        return [
            (flat(g, d, t), flat(*move(g, d, t)))
            for g in range(2)
            for d in range(dp_count)
            for t in range(2)
        ]

    shifts = {
        step: table(lambda g, d, t: (g, (d + 2 * step) % dp_count, t))
        for step in range(1, dp_count // 2)
    }
    return shifts | {
        "x": table(lambda g, d, t: (g, d ^ 1, t)),
        "y": table(lambda g, d, t: (g ^ 1, d, t)),
        "t": table(lambda g, d, t: (g, d, t ^ 1)),
        "first": table(lambda g, d, t: (g, d ^ 1, t) if t == 0 else (g ^ 1, d, t)),
        "second": table(lambda g, d, t: (g ^ 1, d, t) if t == 0 else (g, d ^ 1, t)),
    }


def layer(
    inputs,
    cotangent,
    lengths,
    attn_gain,
    w_query,
    b_query,
    w_key,
    b_key,
    w_value,
    b_value,
    w_out,
    ffn_gain,
    w_gate,
    w_up,
    w_down,
):
    bf16 = jnp.bfloat16
    f32 = jnp.float32
    dp_count = lax.axis_size("dp")
    line = dp_count // 2
    dp_index = lax.axis_index("dp")
    x_index = dp_index % 2
    z_index = dp_index // 2
    y_index = lax.axis_index("group")
    core = lax.axis_index("tensor")
    table = routes(dp_count)
    line_groups = [[2 * z + x for z in range(line)] for x in range(2)]
    tokens, d_model = inputs.shape
    half = tokens // 2
    rows = w_query.shape[0]
    head_count = w_query.shape[1] // HD
    kv_count = w_key.shape[1] // HD
    ffn_cols = w_gate.shape[1]
    quarter = -(-ffn_cols // 512) * 128

    def send(value, route):
        return lax.ppermute(value, AXES, table[route])

    def pick(value, index):
        return lax.dynamic_index_in_dim(value, index, 0, keepdims=False)

    def in_order(index, mine, other):
        first = index == 0
        return jnp.where(first, mine, other), jnp.where(first, other, mine)

    def my_half(value):
        return pick(value.reshape(2, half, value.shape[-1]), core)

    def other_half(value):
        return pick(value.reshape(2, half, value.shape[-1]), 1 - core)

    def both_halves(mine):
        return jnp.concatenate(in_order(core, mine, send(mine, "t")), axis=0)

    def after(value, *others):
        return lax.optimization_barrier((value, *others))[0]

    def square_far(mine, near, *others):
        mine_sib = send(mine, "t")
        near_sib = send(near, "t")
        far = send(after(jnp.stack([mine, near]), *others), "second")
        far_sib = send(far, "t")
        whole = jnp.concatenate(
            [mine, near, far[0], far[1], mine_sib, near_sib, far_sib[0], far_sib[1]], axis=0
        )
        return whole, far

    def scatter_far(mine, theirs):
        came = send(theirs, "t")
        total = (mine.astype(f32) + came.astype(f32)).reshape(4, half, d_model)
        return total[:2], send(total[2:].astype(bf16), "second")

    def scatter_near(kept, came):
        total = kept + came.astype(f32)
        came = send(total[1].astype(bf16), "first")
        return total[0] + came.astype(f32)

    def ffn_quarter(weight, index):
        parts = [weight[:, i * quarter : (i + 1) * quarter] for i in range(4)]
        parts[3] = jnp.pad(parts[3], ((0, 0), (0, 4 * quarter - ffn_cols)))
        upper = jnp.where(index % 2 == 0, parts[2], parts[3])
        lower = jnp.where(index % 2 == 0, parts[0], parts[1])
        return jnp.where(index < 2, lower, upper)

    def ffn_pair(weights):
        other = [ffn_quarter(w, (1 - x_index) * 2 + y_index) for w in weights]
        came = send(jnp.concatenate(other, axis=1), "x")
        mine = [ffn_quarter(w, x_index * 2 + y_index) for w in weights]
        return jnp.stack(in_order(x_index, jnp.concatenate(mine, axis=1), came))

    def ffn_gather(pair):
        full = lax.all_gather(pair, "dp", axis=0, axis_index_groups=line_groups)
        return full.reshape(d_model, pair.shape[-1])

    def ffn_scatter(grad):
        parts = grad.astype(bf16).reshape(line, 2 * rows, quarter)
        return lax.psum_scatter(
            parts, "dp", scatter_dimension=0, axis_index_groups=line_groups
        ).reshape(2, rows, quarter)

    def ffn_swap(summed, *others):
        came = send(pick(summed, 1 - x_index), "x")
        pair = jnp.stack(in_order(x_index, pick(summed, x_index), came))
        low, high = in_order(y_index, pair, send(after(pair, *others), "y"))
        whole = jnp.concatenate([low[0], high[0], low[1], high[1]], axis=1)
        return whole[:, :ffn_cols].astype(f32)

    cut = line // 2
    part_rows = rows // 2

    def line_sends(weight):
        mine = lax.dynamic_slice_in_dim(weight, y_index * part_rows, part_rows, 0)
        return [mine] + [send(mine, step) for step in range(1, line)]

    def line_join(pieces):
        whole = jnp.zeros((line,) + pieces[0].shape, bf16)
        for step, piece in enumerate(pieces):
            spot = ((z_index - step) % line, 0, 0)
            whole = lax.dynamic_update_slice(whole, piece[None], spot)
        return whole

    def near_sends(blocks):
        low, high = blocks[:cut], blocks[cut:]
        return low, high, send(low, "x"), send(high, "y")

    def far_join(low, high, low_near, high_near):
        low_far = send(jnp.stack([low, low_near]), "y")
        high_far = send(jnp.stack([high, high_near]), "x")
        cols = low.shape[-1]
        whole = jnp.zeros((line, 2, 2, part_rows, cols), bf16)
        x, y = x_index, y_index
        for piece, z, px, py in (
            (low, 0, x, y),
            (low_near, 0, 1 - x, y),
            (low_far[0], 0, x, 1 - y),
            (low_far[1], 0, 1 - x, 1 - y),
            (high, cut, x, y),
            (high_near, cut, x, 1 - y),
            (high_far[0], cut, 1 - x, y),
            (high_far[1], cut, 1 - x, 1 - y),
        ):
            whole = lax.dynamic_update_slice(whole, piece[:, None, None], (z, px, py, 0, 0))
        return whole.reshape(d_model, cols)

    def take(value, axis, index):
        return lax.dynamic_index_in_dim(value, index, axis, keepdims=False)

    def fold(value, axis, index, route):
        came = send(take(value, axis, 1 - index), route)
        return (take(value, axis, index).astype(f32) + came.astype(f32)).astype(bf16)

    def scatter_hop1(grad):
        view = grad.reshape(line, 2, 2, part_rows, grad.shape[-1])
        low = fold(view[:cut], 1, x_index, "x")
        return low, fold(view[cut:], 2, y_index, "y")

    def scatter_hop2(low, high):
        return jnp.concatenate([fold(low, 1, y_index, "y"), fold(high, 1, x_index, "x")])

    def scatter_line(blocks):
        total = pick(blocks, z_index).astype(f32)
        for step in range(1, line):
            total = total + send(pick(blocks, (z_index + step) % line), step).astype(f32)
        return total.astype(bf16)

    def scatter_end(mine):
        return jnp.concatenate(in_order(y_index, mine, send(mine, "y"))).astype(f32)

    query_cols = head_count * HD
    key_cols = kv_count * HD
    qkv_cols = query_cols + 2 * key_cols
    gains = jnp.pad(jnp.stack([attn_gain, ffn_gain], axis=1), ((0, 0), (0, HD - 2)))

    qkv_pieces = line_sends(jnp.concatenate([w_query, w_key, w_value, gains], axis=1))
    gate_up_pair = ffn_pair([w_gate, w_up])
    gate_up_full = ffn_gather(after(gate_up_pair, *qkv_pieces))
    qkv_near = near_sends(after(line_join(qkv_pieces), gate_up_pair))
    qkv_full = far_join(*qkv_near)
    out_pieces = line_sends(after(w_out, *qkv_near))
    out_near = near_sends(after(line_join(out_pieces), qkv_full))
    out_full = far_join(*out_near)
    down_pair = ffn_pair([after(w_down, out_full)])
    down_full = ffn_gather(after(down_pair, gate_up_pair))
    cot_half = my_half(cotangent)
    cot_near = send(after(cot_half, out_full), "first")

    _, position = layout(lengths[0])
    cosine, sine_table = angles(position)
    sign = jnp.where(jnp.arange(HD) < HD // 2, -1.0, 1.0)
    signed_sine = sine_table * sign
    start = (jnp.arange(SEQ, dtype=jnp.int32) - position)[:, None]
    stream = inputs.astype(f32)
    inv_one = lax.rsqrt(jnp.mean(stream * stream, axis=-1, keepdims=True) + EPSILON)
    qkv_full = after(qkv_full, cosine, signed_sine, start, inv_one)
    gain_one = qkv_full[:, qkv_cols].astype(f32)
    gain_two = qkv_full[:, qkv_cols + 1].astype(f32)
    qkv_full = qkv_full[:, :qkv_cols]

    h_one = (stream * inv_one * gain_one).astype(bf16)
    qkv_bias = jnp.concatenate([b_query, b_key, b_value]).astype(f32)
    qkv_pre = plain_dot(h_one, qkv_full) + qkv_bias
    q_rot, k_rot, v_low, attended, lse = attend(
        after(qkv_pre, *out_near), cosine, signed_sine, start
    )
    branch = trans_dot(attended, out_full)
    resid = (
        my_half(stream)
        + my_half(branch)
        + send(other_half(branch).astype(bf16), "t").astype(f32)
    )
    inv_two = lax.rsqrt(jnp.mean(resid * resid, axis=-1, keepdims=True) + EPSILON)
    norm_two = resid * inv_two
    h_two_half = after((norm_two * gain_two).astype(bf16), cot_near)
    h_two, h_two_far = square_far(h_two_half, send(h_two_half, "first"))
    cot_all, _ = square_far(cot_half, cot_near, h_two_far)

    gate_full = gate_up_full[:, :quarter]
    up_full = gate_up_full[:, quarter:]
    gate_low = plain_dot(h_two, gate_full).astype(bf16)
    up_low = plain_dot(after(h_two, gate_low), up_full).astype(bf16)
    gate_pre = gate_low.astype(f32)
    up_pre = up_low.astype(f32)
    sigmoid_gate = jax.nn.sigmoid(gate_pre)
    swish_gate = gate_pre * sigmoid_gate
    hidden = (swish_gate * up_pre).astype(bf16)
    down_part = outer_dot(cot_all, hidden).astype(bf16)
    down_sum = ffn_scatter(down_part)
    d_hidden = plain_dot(after(cot_all, down_part), down_full)
    d_gate = (d_hidden * up_pre * sigmoid_gate * (1.0 + gate_pre * (1.0 - sigmoid_gate))).astype(
        bf16
    )
    d_up = (d_hidden * swish_gate).astype(bf16)
    mid = 4 * half
    low_hidden = after(hidden, d_gate)
    ffn_theirs = trans_dot(low_hidden[mid:], down_full).astype(bf16)
    gate_part = outer_dot(after(h_two, ffn_theirs), d_gate).astype(bf16)
    gate_sum = ffn_scatter(gate_part)
    ffn_mine = trans_dot(after(low_hidden[:mid], gate_part), down_full).astype(bf16)
    ffn_kept, ffn_came = scatter_far(ffn_mine, ffn_theirs)

    def entry(gate_side, up_side):
        return (trans_dot(gate_side, gate_full) + trans_dot(up_side, up_full)).astype(bf16)

    theirs = entry(after(d_gate[mid:], ffn_mine), after(d_up[mid:], ffn_mine))
    mine = entry(after(d_gate[:mid], theirs), after(d_up[:mid], theirs))
    kept, came = scatter_far(mine, theirs)
    up_part = outer_dot(after(h_two, mine), d_up).astype(bf16)
    up_sum = ffn_scatter(up_part)
    d_h_two = scatter_near(kept, after(came, up_part))
    ffn_total = scatter_near(ffn_kept, after(ffn_came, d_h_two))
    layer_out = both_halves((resid + ffn_total).astype(bf16))

    scaled = d_h_two * gain_two
    d_resid = cot_half.astype(f32) + inv_two * (
        scaled - norm_two * jnp.mean(norm_two * scaled, axis=-1, keepdims=True)
    )
    gain_two_part = jnp.sum(d_h_two * norm_two, axis=0)
    d_out_low = both_halves(d_resid.astype(bf16))
    out_hop = scatter_hop1(outer_dot(d_out_low, attended).astype(bf16))
    down_grad = ffn_swap(down_sum)
    d_attended = plain_dot(d_out_low, out_full).astype(bf16)
    d_qkv = attend_back(q_rot, k_rot, v_low, d_attended, lse, cosine, signed_sine, start)
    qkv_part = outer_dot(after(h_one, *out_hop), d_qkv).astype(bf16)
    qkv_hop = scatter_hop1(qkv_part)
    out_blocks = scatter_hop2(*out_hop)
    qkv_blocks = scatter_hop2(*qkv_hop)
    out_mine = scatter_line(out_blocks)
    qkv_mine = scatter_line(after(qkv_blocks, out_mine))
    out_grad = scatter_end(out_mine)
    qkv_grad = scatter_end(qkv_mine)
    gate_grad = ffn_swap(after(gate_sum, d_out_low), *qkv_hop)
    entry_one = trans_dot(d_qkv, qkv_full)
    d_h_one = my_half(entry_one) + send(other_half(entry_one).astype(bf16), "t").astype(f32)
    half_inv = my_half(inv_one)
    norm_one = my_half(stream) * half_inv
    scaled = d_h_one * gain_one
    input_grad = both_halves(
        (
            d_resid
            + half_inv * (scaled - norm_one * jnp.mean(norm_one * scaled, axis=-1, keepdims=True))
        ).astype(bf16)
    )
    gain_one_part = jnp.sum(d_h_one * norm_one, axis=0)

    bias_part = jnp.sum(d_qkv.astype(f32), axis=0)
    small = jnp.concatenate([gain_one_part, gain_two_part, bias_part]).reshape(-1, 128)
    small = small + send(small, "y")
    step = 1
    while step < dp_count:
        small = small + lax.ppermute(small, "dp", [(i, i ^ step) for i in range(dp_count)])
        step *= 2
    small = small.reshape(-1)
    up_grad = ffn_swap(after(up_sum, gate_grad, qkv_mine, small))
    gain_sums = small[: 2 * d_model].reshape(2, dp_count, rows)
    gain_mine = lax.dynamic_index_in_dim(gain_sums, dp_index, 1, keepdims=False)
    gain_mine = gain_mine + send(gain_mine, "t")
    bias_sum = small[2 * d_model :]
    return (
        layer_out,
        input_grad,
        gain_mine[0],
        qkv_grad[:, :query_cols],
        bias_sum[:query_cols],
        qkv_grad[:, query_cols : query_cols + key_cols],
        bias_sum[query_cols : query_cols + key_cols],
        qkv_grad[:, query_cols + key_cols :],
        bias_sum[query_cols + key_cols :],
        out_grad,
        gain_mine[1],
        gate_grad,
        up_grad,
        down_grad,
    )


def solution(mesh):
    in_specs = (
        P(("group", "dp"), None),
        P(("group", "dp"), None),
        P(("group", "dp"), None),
        P("dp"),
        P("dp", "tensor"),
        P("tensor"),
        P("dp", "tensor"),
        P("tensor"),
        P("dp", "tensor"),
        P("tensor"),
        P("dp", "tensor"),
        P("dp"),
        P("dp", "tensor"),
        P("dp", "tensor"),
        P("dp", "tensor"),
    )
    out_specs = (
        P(("group", "dp"), None),
        P(("group", "dp"), None),
        P("dp"),
        P("dp", "tensor"),
        P("tensor"),
        P("dp", "tensor"),
        P("tensor"),
        P("dp", "tensor"),
        P("tensor"),
        P("dp", "tensor"),
        P("dp"),
        P("dp", "tensor"),
        P("dp", "tensor"),
        P("dp", "tensor"),
    )
    return jax.shard_map(layer, mesh=mesh, in_specs=in_specs, out_specs=out_specs, check_vma=False)
```

```python
import math

import jax
import jax.numpy as jnp
from jax import lax
from jax.experimental import pallas as pl
from jax.experimental.pallas import tpu as pltpu
from jax.sharding import PartitionSpec as P

HD = 128
SEQ = 768
NSEG = 3


EPSILON = 1e-06
THETA = 10000.0
MASKED_SCORE = -1e30


def layout(lengths):
    segment_ends = jnp.cumsum(lengths, axis=-1)
    segment_starts = segment_ends - lengths
    places = jnp.arange(SEQ, dtype=jnp.int32)
    segment = jnp.sum((places[:, None] >= segment_ends[..., None, :]).astype(jnp.int32), axis=-1)
    choose = segment[..., None] == jnp.arange(NSEG, dtype=jnp.int32)
    picked = jnp.sum(jnp.where(choose, segment_starts[..., None, :], 0), axis=-1)
    return (segment, places - picked)


def angles(position):
    frequency = jnp.exp(-(math.log(THETA) * 2.0 / HD) * jnp.arange(HD // 2, dtype=jnp.float32))
    phase_angle = position.astype(jnp.float32)[..., None] * frequency
    phase_angle = jnp.concatenate([phase_angle, phase_angle], axis=-1)
    return (jnp.cos(phase_angle), jnp.sin(phase_angle))


def plain_dot(left_side, right_side):
    return jnp.dot(left_side, right_side, preferred_element_type=jnp.float32)


def trans_dot(left_side, right_side):
    return lax.dot_general(
        left_side, right_side, (((1,), (1,)), ((), ())), preferred_element_type=jnp.float32
    )


def outer_dot(left_side, right_side):
    return lax.dot_general(
        left_side, right_side, (((0,), (0,)), ((), ())), preferred_element_type=jnp.float32
    )


BLOCK = 256


def rotated(values, cosine, signed_sine):
    return values * cosine + pltpu.roll(values, HD // 2, 1) * signed_sine


def unrotated(values, cosine, signed_sine):
    return values * cosine - pltpu.roll(values, HD // 2, 1) * signed_sine


def allowed_block(start, top, width):
    row = top + lax.broadcasted_iota(jnp.int32, (BLOCK, width), 0)
    col = lax.broadcasted_iota(jnp.int32, (BLOCK, width), 1)
    return (col >= start) & (col <= row)


def attend_body(
    q_pre, k_pre, v_pre, cosine, signed_sine, start, q_out, k_out, v_out, att_out, lse_out
):
    head = pl.program_id(0)

    @pl.when(head == 0)
    def _():
        k_out[...] = rotated(k_pre[...], cosine[...], signed_sine[...]).astype(jnp.bfloat16)
        v_out[...] = v_pre[...].astype(jnp.bfloat16)
        lse_out[...] = jnp.zeros_like(lse_out)

    q_out[...] = rotated(q_pre[...], cosine[...], signed_sine[...]).astype(jnp.bfloat16)
    for top in range(0, SEQ, BLOCK):
        width = top + BLOCK
        rows = pl.ds(top, BLOCK)
        scores = trans_dot(q_out[rows, :], k_out[:width, :]) * HD ** (-0.5)
        scores = jnp.where(allowed_block(start[rows, :], top, width), scores, MASKED_SCORE)
        row_max = jnp.max(scores, axis=1, keepdims=True)
        terms = jnp.exp(scores - row_max)
        total = jnp.sum(terms, axis=1, keepdims=True)
        probs = (terms * (1.0 / total)).astype(jnp.bfloat16)
        att_out[rows, :] = plain_dot(probs, v_out[:width, :]).astype(jnp.bfloat16)
        lane = lax.broadcasted_iota(jnp.int32, (BLOCK, HD), 1)
        lse_out[rows, :] = jnp.where(lane == head, row_max + jnp.log(total), lse_out[rows, :])


def attend_back_body(
    q_rot, k_rot, v_low, d_att, lse, cosine, signed_sine, start, grad_out, dk_sum, dv_sum
):
    head = pl.program_id(0)

    @pl.when(head == 0)
    def _():
        dk_sum[...] = jnp.zeros_like(dk_sum)
        dv_sum[...] = jnp.zeros_like(dv_sum)

    for top in range(0, SEQ, BLOCK):
        width = top + BLOCK
        rows = pl.ds(top, BLOCK)
        query = q_rot[rows, :]
        d_out = d_att[rows, :]
        lane = lax.broadcasted_iota(jnp.int32, (BLOCK, HD), 1)
        row_lse = jnp.sum(jnp.where(lane == head, lse[rows, :], 0.0), axis=1, keepdims=True)
        scores = trans_dot(query, k_rot[:width, :]) * HD ** (-0.5)
        scores = jnp.where(allowed_block(start[rows, :], top, width), scores, MASKED_SCORE)
        probs = jnp.exp(scores - row_lse)
        d_probs = trans_dot(d_out, v_low[:width, :])
        inner = jnp.sum(probs * d_probs, axis=1, keepdims=True)
        d_scores = (probs * (d_probs - inner)).astype(jnp.bfloat16)
        d_query = plain_dot(d_scores, k_rot[:width, :]) * HD ** (-0.5)
        d_query = unrotated(d_query, cosine[rows, :], signed_sine[rows, :])
        cols = pl.ds(pl.multiple_of(head * HD, HD), HD)
        grad_out[rows, cols] = d_query.astype(jnp.bfloat16)
        dk_sum[:width, :] += outer_dot(d_scores, query)
        dv_sum[:width, :] += outer_dot(probs.astype(jnp.bfloat16), d_out)

    @pl.when(head == pl.num_programs(0) - 1)
    def _():
        edge = grad_out.shape[1] - 2 * HD
        d_key = unrotated(dk_sum[...] * HD ** (-0.5), cosine[...], signed_sine[...])
        grad_out[:, edge : edge + HD] = d_key.astype(jnp.bfloat16)
        grad_out[:, edge + HD :] = dv_sum[...].astype(jnp.bfloat16)


def fixed(shape):
    return pl.BlockSpec(shape, lambda head: (0, 0))


def column(index):
    return pl.BlockSpec((SEQ, HD), lambda head: (0, index))


PER_HEAD = pl.BlockSpec((SEQ, HD), lambda head: (0, head))
WHOLE = (SEQ, HD)


def attend(qkv_pre, cosine, signed_sine, start):
    heads = qkv_pre.shape[1] // HD - 2
    shape = lambda cols, kind: jax.ShapeDtypeStruct((SEQ, cols), kind)
    low = jnp.bfloat16
    return pl.pallas_call(
        attend_body,
        grid=(heads,),
        in_specs=[PER_HEAD, column(heads), column(heads + 1)]
        + [fixed(WHOLE), fixed(WHOLE), fixed((SEQ, 1))],
        out_specs=[PER_HEAD, fixed(WHOLE), fixed(WHOLE), PER_HEAD, fixed(WHOLE)],
        out_shape=[
            shape(heads * HD, low),
            shape(HD, low),
            shape(HD, low),
            shape(heads * HD, low),
            shape(HD, jnp.float32),
        ],
    )(qkv_pre, qkv_pre, qkv_pre, cosine, signed_sine, start)


def attend_back(q_rot, k_rot, v_low, d_att, lse, cosine, signed_sine, start):
    heads = q_rot.shape[1] // HD
    cols = (heads + 2) * HD
    return pl.pallas_call(
        attend_back_body,
        grid=(heads,),
        in_specs=[PER_HEAD, fixed(WHOLE), fixed(WHOLE), PER_HEAD, fixed(WHOLE)]
        + [fixed(WHOLE), fixed(WHOLE), fixed((SEQ, 1))],
        out_specs=fixed((SEQ, cols)),
        out_shape=jax.ShapeDtypeStruct((SEQ, cols), jnp.bfloat16),
        scratch_shapes=[pltpu.VMEM(WHOLE, jnp.float32), pltpu.VMEM(WHOLE, jnp.float32)],
    )(q_rot, k_rot, v_low, d_att, lse, cosine, signed_sine, start)


AXES = ("group", "dp", "tensor")


def routes(dp_count):
    def table(move):
        flat = lambda g, d, t: (g * dp_count + d) * 2 + t
        return [
            (flat(g, d, t), flat(*move(g, d, t)))
            for g in range(2)
            for d in range(dp_count)
            for t in range(2)
        ]

    shifts = {
        step: table(lambda g, d, t: (g, (d + 2 * step) % dp_count, t))
        for step in range(1, dp_count // 2)
    }
    return shifts | {
        "x": table(lambda g, d, t: (g, d ^ 1, t)),
        "y": table(lambda g, d, t: (g ^ 1, d, t)),
        "t": table(lambda g, d, t: (g, d, t ^ 1)),
        "first": table(lambda g, d, t: (g, d ^ 1, t) if t == 0 else (g ^ 1, d, t)),
        "second": table(lambda g, d, t: (g ^ 1, d, t) if t == 0 else (g, d ^ 1, t)),
    }


def layer(
    inputs,
    cotangent,
    lengths,
    attn_gain,
    w_query,
    b_query,
    w_key,
    b_key,
    w_value,
    b_value,
    w_out,
    ffn_gain,
    w_gate,
    w_up,
    w_down,
):
    bf16 = jnp.bfloat16
    f32 = jnp.float32
    dp_count = lax.axis_size("dp")
    line = dp_count // 2
    dp_index = lax.axis_index("dp")
    x_index = dp_index % 2
    z_index = dp_index // 2
    y_index = lax.axis_index("group")
    core = lax.axis_index("tensor")
    table = routes(dp_count)
    line_groups = [[2 * z + x for z in range(line)] for x in range(2)]
    tokens, d_model = inputs.shape
    half = tokens // 2
    rows = w_query.shape[0]
    head_count = w_query.shape[1] // HD
    kv_count = w_key.shape[1] // HD
    ffn_cols = w_gate.shape[1]
    quarter = -(-ffn_cols // 512) * 128

    def send(value, route):
        return lax.ppermute(value, AXES, table[route])

    def pick(value, index):
        return lax.dynamic_index_in_dim(value, index, 0, keepdims=False)

    def in_order(index, mine, other):
        first = index == 0
        return jnp.where(first, mine, other), jnp.where(first, other, mine)

    def my_half(value):
        return pick(value.reshape(2, half, value.shape[-1]), core)

    def other_half(value):
        return pick(value.reshape(2, half, value.shape[-1]), 1 - core)

    def both_halves(mine):
        return jnp.concatenate(in_order(core, mine, send(mine, "t")), axis=0)

    def square_far(mine, near):
        far = send(jnp.stack([mine, near]), "second")
        mine_sib = send(mine, "t")
        near_sib = send(near, "t")
        far_sib = send(far, "t")
        whole = jnp.concatenate(
            [mine, near, far[0], far[1], mine_sib, near_sib, far_sib[0], far_sib[1]], axis=0
        )
        return whole

    def scatter_far(mine, theirs):
        came = send(theirs, "t")
        total = (mine.astype(f32) + came.astype(f32)).reshape(4, half, d_model)
        return total[:2], send(total[2:].astype(bf16), "second")

    def scatter_near(kept, came):
        total = kept + came.astype(f32)
        came = send(total[1].astype(bf16), "first")
        return total[0] + came.astype(f32)

    def ffn_quarter(weight, index):
        parts = [weight[:, i * quarter : (i + 1) * quarter] for i in range(4)]
        parts[3] = jnp.pad(parts[3], ((0, 0), (0, 4 * quarter - ffn_cols)))
        upper = jnp.where(index % 2 == 0, parts[2], parts[3])
        lower = jnp.where(index % 2 == 0, parts[0], parts[1])
        return jnp.where(index < 2, lower, upper)

    def ffn_pair(weights):
        other = [ffn_quarter(w, (1 - x_index) * 2 + y_index) for w in weights]
        came = send(jnp.concatenate(other, axis=1), "x")
        mine = [ffn_quarter(w, x_index * 2 + y_index) for w in weights]
        return jnp.stack(in_order(x_index, jnp.concatenate(mine, axis=1), came))

    def ffn_gather(pair):
        full = lax.all_gather(pair, "dp", axis=0, axis_index_groups=line_groups)
        return full.reshape(d_model, pair.shape[-1])

    def ffn_scatter(grad):
        parts = grad.astype(bf16).reshape(line, 2 * rows, quarter)
        return lax.psum_scatter(
            parts, "dp", scatter_dimension=0, axis_index_groups=line_groups
        ).reshape(2, rows, quarter)

    def ffn_swap(summed):
        came = send(pick(summed, 1 - x_index), "x")
        pair = jnp.stack(in_order(x_index, pick(summed, x_index), came))
        low, high = in_order(y_index, pair, send(pair, "y"))
        whole = jnp.concatenate([low[0], high[0], low[1], high[1]], axis=1)
        return whole[:, :ffn_cols].astype(f32)

    cut = line // 2
    part_rows = rows // 2

    def line_sends(weight):
        mine = lax.dynamic_slice_in_dim(weight, y_index * part_rows, part_rows, 0)
        return [mine] + [send(mine, step) for step in range(1, line)]

    def line_join(pieces):
        whole = jnp.zeros((line,) + pieces[0].shape, bf16)
        for step, piece in enumerate(pieces):
            spot = ((z_index - step) % line, 0, 0)
            whole = lax.dynamic_update_slice(whole, piece[None], spot)
        return whole

    def near_sends(blocks):
        low, high = blocks[:cut], blocks[cut:]
        return low, high, send(low, "x"), send(high, "y")

    def far_join(low, high, low_near, high_near):
        low_far = send(jnp.stack([low, low_near]), "y")
        high_far = send(jnp.stack([high, high_near]), "x")
        cols = low.shape[-1]
        whole = jnp.zeros((line, 2, 2, part_rows, cols), bf16)
        x, y = x_index, y_index
        for piece, z, px, py in (
            (low, 0, x, y),
            (low_near, 0, 1 - x, y),
            (low_far[0], 0, x, 1 - y),
            (low_far[1], 0, 1 - x, 1 - y),
            (high, cut, x, y),
            (high_near, cut, x, 1 - y),
            (high_far[0], cut, 1 - x, y),
            (high_far[1], cut, 1 - x, 1 - y),
        ):
            whole = lax.dynamic_update_slice(whole, piece[:, None, None], (z, px, py, 0, 0))
        return whole.reshape(d_model, cols)

    def take(value, axis, index):
        return lax.dynamic_index_in_dim(value, index, axis, keepdims=False)

    def fold(value, axis, index, route):
        came = send(take(value, axis, 1 - index), route)
        return (take(value, axis, index).astype(f32) + came.astype(f32)).astype(bf16)

    def scatter_hop1(grad):
        view = grad.reshape(line, 2, 2, part_rows, grad.shape[-1])
        low = fold(view[:cut], 1, x_index, "x")
        return low, fold(view[cut:], 2, y_index, "y")

    def scatter_hop2(low, high):
        low = fold(low, 1, y_index, "y")
        return jnp.concatenate([low, fold(high, 1, x_index, "x")])

    def scatter_line(blocks):
        total = pick(blocks, z_index).astype(f32)
        for step in range(1, line):
            total = total + send(pick(blocks, (z_index + step) % line), step).astype(f32)
        return total.astype(bf16)

    def scatter_end(mine):
        return jnp.concatenate(in_order(y_index, mine, send(mine, "y"))).astype(f32)

    query_cols = head_count * HD
    key_cols = kv_count * HD
    qkv_cols = query_cols + 2 * key_cols
    gains = jnp.pad(jnp.stack([attn_gain, ffn_gain], axis=1), ((0, 0), (0, HD - 2)))

    qkv_weights = jnp.concatenate([w_query, w_key, w_value, gains], axis=1)
    qkv_pieces = line_sends(qkv_weights)
    gate_up_pair = ffn_pair([w_gate, w_up])
    down_pair = ffn_pair([w_down])
    gate_up_full = ffn_gather(gate_up_pair)
    down_full = ffn_gather(down_pair)
    qkv_near = near_sends(line_join(qkv_pieces))
    qkv_full = far_join(*qkv_near)
    out_near = near_sends(line_join(line_sends(w_out)))
    out_full = far_join(*out_near)
    cot_half = my_half(cotangent)
    cot_near = send(cot_half, "first")

    _, position = layout(lengths[0])
    cosine, sine_table = angles(position)
    sign = jnp.where(jnp.arange(HD) < HD // 2, -1.0, 1.0)
    signed_sine = sine_table * sign
    start = (jnp.arange(SEQ, dtype=jnp.int32) - position)[:, None]
    stream = inputs.astype(f32)
    inv_one = lax.rsqrt(jnp.mean(stream * stream, axis=-1, keepdims=True) + EPSILON)
    gain_one = qkv_full[:, qkv_cols].astype(f32)
    gain_two = qkv_full[:, qkv_cols + 1].astype(f32)
    qkv_full = qkv_full[:, :qkv_cols]

    h_one = (stream * inv_one * gain_one).astype(bf16)
    qkv_bias = jnp.concatenate([b_query, b_key, b_value]).astype(f32)
    qkv_pre = plain_dot(h_one, qkv_full) + qkv_bias
    q_rot, k_rot, v_low, attended, lse = attend(qkv_pre, cosine, signed_sine, start)
    branch = trans_dot(attended, out_full)
    resid = (
        my_half(stream)
        + my_half(branch)
        + send(other_half(branch).astype(bf16), "t").astype(f32)
    )
    inv_two = lax.rsqrt(jnp.mean(resid * resid, axis=-1, keepdims=True) + EPSILON)
    norm_two = resid * inv_two
    h_two_half = (norm_two * gain_two).astype(bf16)
    h_two = square_far(h_two_half, send(h_two_half, "first"))
    cot_all = square_far(cot_half, cot_near)

    gate_full = gate_up_full[:, :quarter]
    up_full = gate_up_full[:, quarter:]
    gate_low = plain_dot(h_two, gate_full).astype(bf16)
    up_low = plain_dot(h_two, up_full).astype(bf16)
    gate_pre = gate_low.astype(f32)
    up_pre = up_low.astype(f32)
    sigmoid_gate = jax.nn.sigmoid(gate_pre)
    swish_gate = gate_pre * sigmoid_gate
    hidden = (swish_gate * up_pre).astype(bf16)
    down_part = outer_dot(cot_all, hidden).astype(bf16)
    down_sum = ffn_scatter(down_part)
    late_cot, _ = lax.optimization_barrier((cot_all, down_part))
    d_hidden = plain_dot(late_cot, down_full)
    slope = sigmoid_gate * (1.0 + gate_pre * (1.0 - sigmoid_gate))
    d_gate = (d_hidden * up_pre * slope).astype(bf16)
    d_up = (d_hidden * swish_gate).astype(bf16)
    mid = 4 * half
    ffn_theirs = trans_dot(hidden[mid:], down_full).astype(bf16)
    gate_part = outer_dot(h_two, d_gate).astype(bf16)
    gate_sum = ffn_scatter(gate_part)
    ffn_mine = trans_dot(hidden[:mid], down_full).astype(bf16)
    ffn_kept, ffn_came = scatter_far(ffn_mine, ffn_theirs)

    def entry(gate_side, up_side):
        return (trans_dot(gate_side, gate_full) + trans_dot(up_side, up_full)).astype(bf16)

    theirs = entry(d_gate[mid:], d_up[mid:])
    mine = entry(d_gate[:mid], d_up[:mid])
    kept, came = scatter_far(mine, theirs)
    up_part = outer_dot(h_two, d_up).astype(bf16)
    up_sum = ffn_scatter(up_part)
    d_h_two = scatter_near(kept, came)
    ffn_total = scatter_near(ffn_kept, ffn_came)
    scaled = d_h_two * gain_two
    d_resid = cot_half.astype(f32) + inv_two * (
        scaled - norm_two * jnp.mean(norm_two * scaled, axis=-1, keepdims=True)
    )
    gain_two_part = jnp.sum(d_h_two * norm_two, axis=0)
    d_out_low = both_halves(d_resid.astype(bf16))
    late_resid, _ = lax.optimization_barrier((resid, d_out_low))
    layer_out = both_halves((late_resid + ffn_total).astype(bf16))
    out_part = outer_dot(d_out_low, attended).astype(bf16)
    out_hop = scatter_hop1(out_part)
    down_grad = ffn_swap(down_sum)
    d_attended = plain_dot(d_out_low, out_full).astype(bf16)
    d_qkv = attend_back(q_rot, k_rot, v_low, d_attended, lse, cosine, signed_sine, start)
    qkv_part = outer_dot(h_one, d_qkv).astype(bf16)
    qkv_hop = scatter_hop1(qkv_part)
    out_blocks = scatter_hop2(*out_hop)
    qkv_blocks = scatter_hop2(*qkv_hop)
    out_mine = scatter_line(out_blocks)
    qkv_mine = scatter_line(qkv_blocks)
    out_grad = scatter_end(out_mine)
    qkv_grad = scatter_end(qkv_mine)
    gate_grad = ffn_swap(gate_sum)
    entry_one = trans_dot(d_qkv, qkv_full)
    came = send(other_half(entry_one).astype(bf16), "t")
    d_h_one = my_half(entry_one) + came.astype(f32)
    half_inv = my_half(inv_one)
    norm_one = my_half(stream) * half_inv
    scaled = d_h_one * gain_one
    input_grad = both_halves(
        (
            d_resid
            + half_inv * (scaled - norm_one * jnp.mean(norm_one * scaled, axis=-1, keepdims=True))
        ).astype(bf16),
    )
    gain_one_part = jnp.sum(d_h_one * norm_one, axis=0)

    bias_part = jnp.sum(d_qkv.astype(f32), axis=0)
    small = jnp.concatenate([gain_one_part, gain_two_part, bias_part]).reshape(-1, 128)
    small = small + send(small, "y")
    step = 1
    while step < dp_count:
        small = small + lax.ppermute(small, "dp", [(i, i ^ step) for i in range(dp_count)])
        step *= 2
    small = small.reshape(-1)
    up_grad = ffn_swap(up_sum)
    gain_sums = small[: 2 * d_model].reshape(2, dp_count, rows)
    gain_mine = lax.dynamic_index_in_dim(gain_sums, dp_index, 1, keepdims=False)
    gain_mine = gain_mine + send(gain_mine, "t")
    bias_sum = small[2 * d_model :]
    return (
        layer_out,
        input_grad,
        gain_mine[0],
        qkv_grad[:, :query_cols],
        bias_sum[:query_cols],
        qkv_grad[:, query_cols : query_cols + key_cols],
        bias_sum[query_cols : query_cols + key_cols],
        qkv_grad[:, query_cols + key_cols :],
        bias_sum[query_cols + key_cols :],
        out_grad,
        gain_mine[1],
        gate_grad,
        up_grad,
        down_grad,
    )


def solution(mesh):
    in_specs = (
        P(("group", "dp"), None),
        P(("group", "dp"), None),
        P(("group", "dp"), None),
        P("dp"),
        P("dp", "tensor"),
        P("tensor"),
        P("dp", "tensor"),
        P("tensor"),
        P("dp", "tensor"),
        P("tensor"),
        P("dp", "tensor"),
        P("dp"),
        P("dp", "tensor"),
        P("dp", "tensor"),
        P("dp", "tensor"),
    )
    out_specs = (
        P(("group", "dp"), None),
        P(("group", "dp"), None),
        P("dp"),
        P("dp", "tensor"),
        P("tensor"),
        P("dp", "tensor"),
        P("tensor"),
        P("dp", "tensor"),
        P("tensor"),
        P("dp", "tensor"),
        P("dp"),
        P("dp", "tensor"),
        P("dp", "tensor"),
        P("dp", "tensor"),
    )
    return jax.shard_map(layer, mesh=mesh, in_specs=in_specs, out_specs=out_specs, check_vma=False)
```

```python
import math

import jax
import jax.numpy as jnp
from jax import lax
from jax.experimental import pallas as pl
from jax.experimental.pallas import tpu as pltpu
from jax.sharding import PartitionSpec as P

HD = 128
SEQ = 768
NSEG = 3


EPSILON = 1e-06
THETA = 10000.0
MASKED_SCORE = -1e30


def layout(lengths):
    segment_ends = jnp.cumsum(lengths, axis=-1)
    segment_starts = segment_ends - lengths
    places = jnp.arange(SEQ, dtype=jnp.int32)
    segment = jnp.sum((places[:, None] >= segment_ends[..., None, :]).astype(jnp.int32), axis=-1)
    choose = segment[..., None] == jnp.arange(NSEG, dtype=jnp.int32)
    picked = jnp.sum(jnp.where(choose, segment_starts[..., None, :], 0), axis=-1)
    return (segment, places - picked)


def angles(position):
    frequency = jnp.exp(-(math.log(THETA) * 2.0 / HD) * jnp.arange(HD // 2, dtype=jnp.float32))
    phase_angle = position.astype(jnp.float32)[..., None] * frequency
    phase_angle = jnp.concatenate([phase_angle, phase_angle], axis=-1)
    return (jnp.cos(phase_angle), jnp.sin(phase_angle))


def plain_dot(left_side, right_side):
    return jnp.dot(left_side, right_side, preferred_element_type=jnp.float32)


def trans_dot(left_side, right_side):
    return lax.dot_general(
        left_side, right_side, (((1,), (1,)), ((), ())), preferred_element_type=jnp.float32
    )


def outer_dot(left_side, right_side):
    return lax.dot_general(
        left_side, right_side, (((0,), (0,)), ((), ())), preferred_element_type=jnp.float32
    )


BLOCK = 256


def rotated(values, cosine, signed_sine):
    return values * cosine + pltpu.roll(values, HD // 2, 1) * signed_sine


def unrotated(values, cosine, signed_sine):
    return values * cosine - pltpu.roll(values, HD // 2, 1) * signed_sine


def allowed_block(start, top, width):
    row = top + lax.broadcasted_iota(jnp.int32, (BLOCK, width), 0)
    col = lax.broadcasted_iota(jnp.int32, (BLOCK, width), 1)
    return (col >= start) & (col <= row)


def attend_body(
    q_pre, k_pre, v_pre, cosine, signed_sine, start, q_out, k_out, v_out, att_out, lse_out
):
    head = pl.program_id(0)

    @pl.when(head == 0)
    def _():
        k_out[...] = rotated(k_pre[...], cosine[...], signed_sine[...]).astype(jnp.bfloat16)
        v_out[...] = v_pre[...].astype(jnp.bfloat16)
        lse_out[...] = jnp.zeros_like(lse_out)

    q_out[...] = rotated(q_pre[...], cosine[...], signed_sine[...]).astype(jnp.bfloat16)
    for top in range(0, SEQ, BLOCK):
        width = top + BLOCK
        rows = pl.ds(top, BLOCK)
        scores = trans_dot(q_out[rows, :], k_out[:width, :]) * HD ** (-0.5)
        scores = jnp.where(allowed_block(start[rows, :], top, width), scores, MASKED_SCORE)
        row_max = jnp.max(scores, axis=1, keepdims=True)
        terms = jnp.exp(scores - row_max)
        total = jnp.sum(terms, axis=1, keepdims=True)
        probs = (terms * (1.0 / total)).astype(jnp.bfloat16)
        att_out[rows, :] = plain_dot(probs, v_out[:width, :]).astype(jnp.bfloat16)
        lane = lax.broadcasted_iota(jnp.int32, (BLOCK, HD), 1)
        lse_out[rows, :] = jnp.where(lane == head, row_max + jnp.log(total), lse_out[rows, :])


def attend_back_body(
    q_rot, k_rot, v_low, d_att, lse, cosine, signed_sine, start, grad_out, dk_sum, dv_sum
):
    head = pl.program_id(0)

    @pl.when(head == 0)
    def _():
        dk_sum[...] = jnp.zeros_like(dk_sum)
        dv_sum[...] = jnp.zeros_like(dv_sum)

    for top in range(0, SEQ, BLOCK):
        width = top + BLOCK
        rows = pl.ds(top, BLOCK)
        query = q_rot[rows, :]
        d_out = d_att[rows, :]
        lane = lax.broadcasted_iota(jnp.int32, (BLOCK, HD), 1)
        row_lse = jnp.sum(jnp.where(lane == head, lse[rows, :], 0.0), axis=1, keepdims=True)
        scores = trans_dot(query, k_rot[:width, :]) * HD ** (-0.5)
        scores = jnp.where(allowed_block(start[rows, :], top, width), scores, MASKED_SCORE)
        probs = jnp.exp(scores - row_lse)
        d_probs = trans_dot(d_out, v_low[:width, :])
        inner = jnp.sum(probs * d_probs, axis=1, keepdims=True)
        d_scores = (probs * (d_probs - inner)).astype(jnp.bfloat16)
        d_query = plain_dot(d_scores, k_rot[:width, :]) * HD ** (-0.5)
        d_query = unrotated(d_query, cosine[rows, :], signed_sine[rows, :])
        cols = pl.ds(pl.multiple_of(head * HD, HD), HD)
        grad_out[rows, cols] = d_query.astype(jnp.bfloat16)
        dk_sum[:width, :] += outer_dot(d_scores, query)
        dv_sum[:width, :] += outer_dot(probs.astype(jnp.bfloat16), d_out)

    @pl.when(head == pl.num_programs(0) - 1)
    def _():
        edge = grad_out.shape[1] - 2 * HD
        d_key = unrotated(dk_sum[...] * HD ** (-0.5), cosine[...], signed_sine[...])
        grad_out[:, edge : edge + HD] = d_key.astype(jnp.bfloat16)
        grad_out[:, edge + HD :] = dv_sum[...].astype(jnp.bfloat16)


def fixed(shape):
    return pl.BlockSpec(shape, lambda head: (0, 0))


def column(index):
    return pl.BlockSpec((SEQ, HD), lambda head: (0, index))


PER_HEAD = pl.BlockSpec((SEQ, HD), lambda head: (0, head))
WHOLE = (SEQ, HD)


def attend(qkv_pre, cosine, signed_sine, start):
    heads = qkv_pre.shape[1] // HD - 2
    shape = lambda cols, kind: jax.ShapeDtypeStruct((SEQ, cols), kind)
    low = jnp.bfloat16
    return pl.pallas_call(
        attend_body,
        grid=(heads,),
        in_specs=[PER_HEAD, column(heads), column(heads + 1)]
        + [fixed(WHOLE), fixed(WHOLE), fixed((SEQ, 1))],
        out_specs=[PER_HEAD, fixed(WHOLE), fixed(WHOLE), PER_HEAD, fixed(WHOLE)],
        out_shape=[
            shape(heads * HD, low),
            shape(HD, low),
            shape(HD, low),
            shape(heads * HD, low),
            shape(HD, jnp.float32),
        ],
    )(qkv_pre, qkv_pre, qkv_pre, cosine, signed_sine, start)


def attend_back(q_rot, k_rot, v_low, d_att, lse, cosine, signed_sine, start):
    heads = q_rot.shape[1] // HD
    cols = (heads + 2) * HD
    return pl.pallas_call(
        attend_back_body,
        grid=(heads,),
        in_specs=[PER_HEAD, fixed(WHOLE), fixed(WHOLE), PER_HEAD, fixed(WHOLE)]
        + [fixed(WHOLE), fixed(WHOLE), fixed((SEQ, 1))],
        out_specs=fixed((SEQ, cols)),
        out_shape=jax.ShapeDtypeStruct((SEQ, cols), jnp.bfloat16),
        scratch_shapes=[pltpu.VMEM(WHOLE, jnp.float32), pltpu.VMEM(WHOLE, jnp.float32)],
    )(q_rot, k_rot, v_low, d_att, lse, cosine, signed_sine, start)


AXES = ("group", "dp", "tensor")


def routes(dp_count):
    def table(move):
        flat = lambda g, d, t: (g * dp_count + d) * 2 + t
        return [
            (flat(g, d, t), flat(*move(g, d, t)))
            for g in range(2)
            for d in range(dp_count)
            for t in range(2)
        ]

    shifts = {
        step: table(lambda g, d, t: (g, (d + 2 * step) % dp_count, t))
        for step in range(1, dp_count // 2)
    }
    return shifts | {
        "x": table(lambda g, d, t: (g, d ^ 1, t)),
        "y": table(lambda g, d, t: (g ^ 1, d, t)),
        "t": table(lambda g, d, t: (g, d, t ^ 1)),
        "first": table(lambda g, d, t: (g, d ^ 1, t) if t == 0 else (g ^ 1, d, t)),
        "second": table(lambda g, d, t: (g ^ 1, d, t) if t == 0 else (g, d ^ 1, t)),
    }


def layer(
    inputs,
    cotangent,
    lengths,
    attn_gain,
    w_query,
    b_query,
    w_key,
    b_key,
    w_value,
    b_value,
    w_out,
    ffn_gain,
    w_gate,
    w_up,
    w_down,
):
    bf16 = jnp.bfloat16
    f32 = jnp.float32
    dp_count = lax.axis_size("dp")
    line = dp_count // 2
    dp_index = lax.axis_index("dp")
    x_index = dp_index % 2
    z_index = dp_index // 2
    y_index = lax.axis_index("group")
    core = lax.axis_index("tensor")
    table = routes(dp_count)
    line_groups = [[2 * z + x for z in range(line)] for x in range(2)]
    tokens, d_model = inputs.shape
    half = tokens // 2
    rows = w_query.shape[0]
    head_count = w_query.shape[1] // HD
    kv_count = w_key.shape[1] // HD
    ffn_cols = w_gate.shape[1]
    quarter = -(-ffn_cols // 512) * 128

    def send(value, route):
        return lax.ppermute(value, AXES, table[route])

    def pick(value, index):
        return lax.dynamic_index_in_dim(value, index, 0, keepdims=False)

    def in_order(index, mine, other):
        first = index == 0
        return jnp.where(first, mine, other), jnp.where(first, other, mine)

    def my_half(value):
        return pick(value.reshape(2, half, value.shape[-1]), core)

    def other_half(value):
        return pick(value.reshape(2, half, value.shape[-1]), 1 - core)

    def both_halves(mine):
        return jnp.concatenate(in_order(core, mine, send(mine, "t")), axis=0)

    def square_far(mine, near):
        far = send(jnp.stack([mine, near]), "second")
        mine_sib = send(mine, "t")
        near_sib = send(near, "t")
        far_sib = send(far, "t")
        whole = jnp.concatenate(
            [mine, near, far[0], far[1], mine_sib, near_sib, far_sib[0], far_sib[1]], axis=0
        )
        return whole

    quad = 2 * half

    def scatter_far(product, theirs):
        came = send(theirs, "t")
        far = product(slice(quad, 2 * quad)) + came[quad:].astype(f32)
        far = far.astype(bf16).reshape(2, half, d_model)
        came_far = send(far, "second")
        kept = product(slice(0, quad)) + came[:quad].astype(f32)
        return kept.reshape(2, half, d_model), came_far

    def scatter_near(kept, came):
        near = (kept[1] + came[1].astype(f32)).astype(bf16)
        came_near = send(near, "first")
        return kept[0] + came[0].astype(f32) + came_near.astype(f32)

    def ffn_quarter(weight, index):
        parts = [weight[:, i * quarter : (i + 1) * quarter] for i in range(4)]
        parts[3] = jnp.pad(parts[3], ((0, 0), (0, 4 * quarter - ffn_cols)))
        upper = jnp.where(index % 2 == 0, parts[2], parts[3])
        lower = jnp.where(index % 2 == 0, parts[0], parts[1])
        return jnp.where(index < 2, lower, upper)

    def ffn_pair(weights):
        other = [ffn_quarter(w, (1 - x_index) * 2 + y_index) for w in weights]
        came = send(jnp.concatenate(other, axis=1), "x")
        mine = [ffn_quarter(w, x_index * 2 + y_index) for w in weights]
        return jnp.stack(in_order(x_index, jnp.concatenate(mine, axis=1), came))

    def ffn_gather(pair):
        full = lax.all_gather(pair, "dp", axis=0, axis_index_groups=line_groups)
        return full.reshape(d_model, pair.shape[-1])

    def ffn_scatter(grad):
        parts = grad.astype(bf16).reshape(line, 2 * rows, quarter)
        return lax.psum_scatter(
            parts, "dp", scatter_dimension=0, axis_index_groups=line_groups
        ).reshape(2, rows, quarter)

    def ffn_swap(summed):
        came = send(pick(summed, 1 - x_index), "x")
        pair = jnp.stack(in_order(x_index, pick(summed, x_index), came))
        low, high = in_order(y_index, pair, send(pair, "y"))
        whole = jnp.concatenate([low[0], high[0], low[1], high[1]], axis=1)
        return whole[:, :ffn_cols].astype(f32)

    cut = line // 2
    part_rows = rows // 2

    def line_sends(weight):
        mine = lax.dynamic_slice_in_dim(weight, y_index * part_rows, part_rows, 0)
        return [mine] + [send(mine, step) for step in range(1, line)]

    def line_join(pieces):
        whole = jnp.zeros((line,) + pieces[0].shape, bf16)
        for step, piece in enumerate(pieces):
            spot = ((z_index - step) % line, 0, 0)
            whole = lax.dynamic_update_slice(whole, piece[None], spot)
        return whole

    def near_sends(blocks):
        low, high = blocks[:cut], blocks[cut:]
        return low, high, send(low, "x"), send(high, "y")

    def far_join(low, high, low_near, high_near):
        low_far = send(jnp.stack([low, low_near]), "y")
        high_far = send(jnp.stack([high, high_near]), "x")
        cols = low.shape[-1]
        whole = jnp.zeros((line, 2, 2, part_rows, cols), bf16)
        x, y = x_index, y_index
        for piece, z, px, py in (
            (low, 0, x, y),
            (low_near, 0, 1 - x, y),
            (low_far[0], 0, x, 1 - y),
            (low_far[1], 0, 1 - x, 1 - y),
            (high, cut, x, y),
            (high_near, cut, x, 1 - y),
            (high_far[0], cut, 1 - x, y),
            (high_far[1], cut, 1 - x, 1 - y),
        ):
            whole = lax.dynamic_update_slice(whole, piece[:, None, None], (z, px, py, 0, 0))
        return whole.reshape(d_model, cols)

    def take(value, axis, index):
        return lax.dynamic_index_in_dim(value, index, axis, keepdims=False)

    def fold(value, axis, index, route):
        came = send(take(value, axis, 1 - index), route)
        return (take(value, axis, index).astype(f32) + came.astype(f32)).astype(bf16)

    def scatter_hop1(grad):
        view = grad.reshape(line, 2, 2, part_rows, grad.shape[-1])
        low = fold(view[:cut], 1, x_index, "x")
        return low, fold(view[cut:], 2, y_index, "y")

    def scatter_hop2(low, high):
        low = fold(low, 1, y_index, "y")
        return jnp.concatenate([low, fold(high, 1, x_index, "x")])

    def scatter_line(blocks):
        total = pick(blocks, z_index).astype(f32)
        for step in range(1, line):
            total = total + send(pick(blocks, (z_index + step) % line), step).astype(f32)
        return total.astype(bf16)

    def scatter_end(mine):
        return jnp.concatenate(in_order(y_index, mine, send(mine, "y"))).astype(f32)

    query_cols = head_count * HD
    key_cols = kv_count * HD
    qkv_cols = query_cols + 2 * key_cols
    gains = jnp.pad(jnp.stack([attn_gain, ffn_gain], axis=1), ((0, 0), (0, HD - 2)))

    qkv_weights = jnp.concatenate([w_query, w_key, w_value, gains], axis=1)
    qkv_pieces = line_sends(qkv_weights)
    gate_up_pair = ffn_pair([w_gate, w_up])
    down_pair = ffn_pair([w_down])
    gate_up_full = ffn_gather(gate_up_pair)
    down_full = ffn_gather(down_pair)
    qkv_near = near_sends(line_join(qkv_pieces))
    qkv_full = far_join(*qkv_near)
    out_near = near_sends(line_join(line_sends(w_out)))
    out_full = far_join(*out_near)
    cot_half = my_half(cotangent)
    cot_near = send(cot_half, "first")

    _, position = layout(lengths[0])
    cosine, sine_table = angles(position)
    sign = jnp.where(jnp.arange(HD) < HD // 2, -1.0, 1.0)
    signed_sine = sine_table * sign
    start = (jnp.arange(SEQ, dtype=jnp.int32) - position)[:, None]
    stream = inputs.astype(f32)
    inv_one = lax.rsqrt(jnp.mean(stream * stream, axis=-1, keepdims=True) + EPSILON)
    gain_one = qkv_full[:, qkv_cols].astype(f32)
    gain_two = qkv_full[:, qkv_cols + 1].astype(f32)
    qkv_full = qkv_full[:, :qkv_cols]

    h_one = (stream * inv_one * gain_one).astype(bf16)
    qkv_bias = jnp.concatenate([b_query, b_key, b_value]).astype(f32)
    qkv_pre = plain_dot(h_one, qkv_full) + qkv_bias
    q_rot, k_rot, v_low, attended, lse = attend(qkv_pre, cosine, signed_sine, start)
    branch = trans_dot(attended, out_full)
    resid = (
        my_half(stream)
        + my_half(branch)
        + send(other_half(branch).astype(bf16), "t").astype(f32)
    )
    inv_two = lax.rsqrt(jnp.mean(resid * resid, axis=-1, keepdims=True) + EPSILON)
    norm_two = resid * inv_two
    h_two_half = (norm_two * gain_two).astype(bf16)
    h_two = square_far(h_two_half, send(h_two_half, "first"))
    cot_all = square_far(cot_half, cot_near)

    gate_full = gate_up_full[:, :quarter]
    up_full = gate_up_full[:, quarter:]
    gate_low = plain_dot(h_two, gate_full).astype(bf16)
    up_low = plain_dot(h_two, up_full).astype(bf16)
    gate_pre = gate_low.astype(f32)
    up_pre = up_low.astype(f32)
    sigmoid_gate = jax.nn.sigmoid(gate_pre)
    swish_gate = gate_pre * sigmoid_gate
    hidden = (swish_gate * up_pre).astype(bf16)
    down_part = outer_dot(cot_all, hidden).astype(bf16)
    down_sum = ffn_scatter(down_part)
    late_cot, _ = lax.optimization_barrier((cot_all, down_part))
    d_hidden = plain_dot(late_cot, down_full)
    slope = sigmoid_gate * (1.0 + gate_pre * (1.0 - sigmoid_gate))
    d_gate = (d_hidden * up_pre * slope).astype(bf16)
    d_up = (d_hidden * swish_gate).astype(bf16)
    mid = 4 * half
    ffn_theirs = trans_dot(hidden[mid:], down_full).astype(bf16)
    gate_part = outer_dot(h_two, d_gate).astype(bf16)
    gate_sum = ffn_scatter(gate_part)
    ffn_kept, ffn_came = scatter_far(lambda part: trans_dot(hidden[part], down_full), ffn_theirs)

    def entry(part):
        return trans_dot(d_gate[part], gate_full) + trans_dot(d_up[part], up_full)

    theirs = entry(slice(mid, 2 * mid)).astype(bf16)
    kept, came = scatter_far(entry, theirs)
    up_part = outer_dot(h_two, d_up).astype(bf16)
    up_sum = ffn_scatter(up_part)
    d_h_two = scatter_near(kept, came)
    ffn_total = scatter_near(ffn_kept, ffn_came)
    scaled = d_h_two * gain_two
    d_resid = cot_half.astype(f32) + inv_two * (
        scaled - norm_two * jnp.mean(norm_two * scaled, axis=-1, keepdims=True)
    )
    gain_two_part = jnp.sum(d_h_two * norm_two, axis=0)
    d_out_low = both_halves(d_resid.astype(bf16))
    late_resid, _ = lax.optimization_barrier((resid, d_out_low))
    layer_out = both_halves((late_resid + ffn_total).astype(bf16))
    out_part = outer_dot(d_out_low, attended).astype(bf16)
    out_hop = scatter_hop1(out_part)
    down_grad = ffn_swap(down_sum)
    d_attended = plain_dot(d_out_low, out_full).astype(bf16)
    d_qkv = attend_back(q_rot, k_rot, v_low, d_attended, lse, cosine, signed_sine, start)
    qkv_part = outer_dot(h_one, d_qkv).astype(bf16)
    qkv_hop = scatter_hop1(qkv_part)
    out_blocks = scatter_hop2(*out_hop)
    qkv_blocks = scatter_hop2(*qkv_hop)
    out_mine = scatter_line(out_blocks)
    qkv_mine = scatter_line(qkv_blocks)
    out_grad = scatter_end(out_mine)
    qkv_grad = scatter_end(qkv_mine)
    gate_grad = ffn_swap(gate_sum)
    entry_one = trans_dot(d_qkv, qkv_full)
    came = send(other_half(entry_one).astype(bf16), "t")
    d_h_one = my_half(entry_one) + came.astype(f32)
    half_inv = my_half(inv_one)
    norm_one = my_half(stream) * half_inv
    scaled = d_h_one * gain_one
    input_grad = both_halves(
        (
            d_resid
            + half_inv * (scaled - norm_one * jnp.mean(norm_one * scaled, axis=-1, keepdims=True))
        ).astype(bf16),
    )
    gain_one_part = jnp.sum(d_h_one * norm_one, axis=0)

    bias_part = jnp.sum(d_qkv.astype(f32), axis=0)
    small = jnp.concatenate([gain_one_part, gain_two_part, bias_part]).reshape(-1, 128)
    small = small + send(small, "y")
    step = 1
    while step < dp_count:
        small = small + lax.ppermute(small, "dp", [(i, i ^ step) for i in range(dp_count)])
        step *= 2
    small = small.reshape(-1)
    up_grad = ffn_swap(up_sum)
    gain_sums = small[: 2 * d_model].reshape(2, dp_count, rows)
    gain_mine = lax.dynamic_index_in_dim(gain_sums, dp_index, 1, keepdims=False)
    gain_mine = gain_mine + send(gain_mine, "t")
    bias_sum = small[2 * d_model :]
    return (
        layer_out,
        input_grad,
        gain_mine[0],
        qkv_grad[:, :query_cols],
        bias_sum[:query_cols],
        qkv_grad[:, query_cols : query_cols + key_cols],
        bias_sum[query_cols : query_cols + key_cols],
        qkv_grad[:, query_cols + key_cols :],
        bias_sum[query_cols + key_cols :],
        out_grad,
        gain_mine[1],
        gate_grad,
        up_grad,
        down_grad,
    )


def solution(mesh):
    in_specs = (
        P(("group", "dp"), None),
        P(("group", "dp"), None),
        P(("group", "dp"), None),
        P("dp"),
        P("dp", "tensor"),
        P("tensor"),
        P("dp", "tensor"),
        P("tensor"),
        P("dp", "tensor"),
        P("tensor"),
        P("dp", "tensor"),
        P("dp"),
        P("dp", "tensor"),
        P("dp", "tensor"),
        P("dp", "tensor"),
    )
    out_specs = (
        P(("group", "dp"), None),
        P(("group", "dp"), None),
        P("dp"),
        P("dp", "tensor"),
        P("tensor"),
        P("dp", "tensor"),
        P("tensor"),
        P("dp", "tensor"),
        P("tensor"),
        P("dp", "tensor"),
        P("dp"),
        P("dp", "tensor"),
        P("dp", "tensor"),
        P("dp", "tensor"),
    )
    return jax.shard_map(layer, mesh=mesh, in_specs=in_specs, out_specs=out_specs, check_vma=False)
```
